32 devices in a mesh: groups: 2 (over y), seq: 16 (over z, x, core).
Axes of the slice: x: 2, y: 2, z: 4, core: 2. Of those that a mesh axis runs over, the one named last changes fastest.
Arguments:
- tokens: bfloat16 [4096, 256], P(('groups', 'seq')), parts along dimension 0, may hold values from -6 to 6
- inv_rms_a: float32 [4096], P(('groups', 'seq')), parts along dimension 0, may hold values from 0.5 to 2
- gain_a: float32 [256], replicated, may hold values from 0.1 to 1.9
- proj_a: bfloat16 [256, 768], replicated, may hold values from -0.375 to 0.375
- taps_a: bfloat16 [128, 256], replicated, may hold values from -0.5 to 0.5
- out_a: bfloat16 [256, 256], replicated, may hold values from -0.375 to 0.375
- inv_rms_b: float32 [4096], P(('groups', 'seq')), parts along dimension 0, may hold values from 0.5 to 2
- gain_b: float32 [256], replicated, may hold values from 0.1 to 1.9
- proj_b: bfloat16 [256, 768], replicated, may hold values from -0.375 to 0.375
- rates_b: float32 [16, 256], replicated, may hold values from 1.4648438e-06 to 0.033
- residues_b: float32 [16, 256], replicated, may hold values from -4 to 4
- out_b: bfloat16 [256, 256], replicated, may hold values from -0.375 to 0.375
Outputs:
- partial_a: bfloat16 [4096, 256], P(('groups', 'seq')), parts along dimension 0
- partial_b: bfloat16 [4096, 256], P(('groups', 'seq')), parts along dimension 0
The draws below stay inside these ranges and needn't reach their ends.
There are 2 independent parts, one for each index of `groups`. The reference program is written for one: setup_inputs(seed, part) draws one part's arguments, and reference() takes and returns one part's arrays. A program takes and returns all parts, laid end to end along the dimension named above; an argument that names none is the same for every part. Nothing has to cross between parts.
All inputs are finite; a program needn't handle non-finite values.
Results may differ from the reference program's by a relative error of at most 0.019.
Values may be sent and summed in bfloat16 or wider, within the bound.
A program may use at most 64 MiB of HBM per device.

```python
import math
import jax
import jax.numpy as jnp
from jax import lax

D = 256
TAPS = 128
MODES = 16
TOKENS = 2048


def block_levels(rng, shape, cuts, least, high):
    def one(position, shards_of):
        draws = jax.random.uniform(jax.random.fold_in(jax.random.fold_in(rng, 6), position), (shards_of,), jnp.float32, least / len(cuts), high / len(cuts))
        return jnp.repeat(jnp.exp(draws), shape[position] // shards_of).reshape((-1,) + (1,) * (len(shape) - position - 1))

    level = one(*cuts[0])
    for cut in cuts[1:]:
        level = level * one(*cut)
    return level


def noise(own_key, shape, deviation, most, split=(), kind=jnp.bfloat16):
    result = jax.random.normal(own_key, shape, jnp.float32) * deviation
    if len(split) > 0:
        result = block_levels(own_key, shape, split, -0.22, 0.18) * result
    return jnp.clip(result, min=-most, max=most).astype(kind)


def setup_inputs(seed: int = 0, part: int = 0) -> dict:
    key_list = jax.random.split(jax.random.key(seed), 13)
    part_splits = jax.random.split(jax.random.fold_in(key_list[12], part), 13)
    return {
        "tokens": noise(part_splits[0], (TOKENS, D), 1.0, 6.0, ((0, 16),)),
        "inv_rms_a": jnp.clip(jnp.exp(math.log(2.0) - 1.3862944 * jax.random.uniform(part_splits[1], (TOKENS,), jnp.float32) ** block_levels(part_splits[1], (TOKENS,), ((0, 16),), -0.2, 0.2)), 0.5, 2.0),
        "gain_a": jnp.clip(1.0 + 0.18 * jax.random.normal(key_list[2], (D,), jnp.float32), 0.1, 1.9),
        "proj_a": noise(key_list[3], (D, 3 * D), D ** -0.5, 0.375),
        "taps_a": noise(key_list[4], (TAPS, D), TAPS ** -0.5, 0.5),
        "out_a": noise(key_list[5], (D, D), D ** -0.5, 0.375),
        "inv_rms_b": jnp.clip(jnp.exp(math.log(2.0) - 1.3862944 * jax.random.uniform(part_splits[6], (TOKENS,), jnp.float32) ** block_levels(part_splits[6], (TOKENS,), ((0, 16),), -0.2, 0.2)), 0.5, 2.0),
        "gain_b": jnp.clip(1.0 + 0.18 * jax.random.normal(key_list[7], (D,), jnp.float32), 0.1, 1.9),
        "proj_b": noise(key_list[8], (D, 3 * D), D ** -0.5, 0.375),
        "rates_b": jnp.clip(jnp.exp(jax.random.uniform(key_list[9], (MODES, D), jnp.float32, math.log(1.4648437627329258e-06), math.log(0.033))), 1.4648437627329258e-06, 0.033),
        "residues_b": noise(key_list[10], (MODES, D), 0.3, 4.0, (), jnp.float32),
        "out_b": noise(key_list[11], (D, D), D ** -0.5, 0.375),
    }


HIGHEST_PREC = lax.Precision.HIGHEST

def rms_scale(values, inv_rms, gain):
    floats = values.astype(jnp.float32)
    return (floats * inv_rms[:, None] * gain).astype(jnp.bfloat16)

def mode_weights(rates, residues, length):
    energy = -jnp.expm1(-2.0 * rates) / -jnp.expm1(-2.0 * rates * length)
    return residues * jnp.sqrt(energy)

def long_filter(rates, residues):
    weights = mode_weights(rates, residues, float(TOKENS))
    positions = jnp.arange(TOKENS).astype(jnp.float32)[:, None]

    def add_mode(totals, mode_pair):
        mode_rate, mode_weight = mode_pair
        return (totals + mode_weight[None, :] * jnp.exp(-mode_rate[None, :] * positions), None)
    return lax.scan(add_mode, jnp.zeros((TOKENS, D), jnp.float32), (rates, weights))[0]

def reference(tokens, inv_rms_a, gain_a, proj_a, taps_a, out_a, inv_rms_b, gain_b, proj_b, rates_b, residues_b, out_b):
    normed = rms_scale(tokens, inv_rms_a, gain_a)
    projected = jnp.dot(normed, proj_a, preferred_element_type=jnp.float32)
    queries = projected[:, :D]
    product = (projected[:, D:2 * D] * projected[:, 2 * D:]).astype(jnp.bfloat16)
    kernel = jnp.flip(taps_a.astype(jnp.float32), 0).T[:, None, :]
    signal_in = product.astype(jnp.float32).T[None]
    short_out = lax.conv_general_dilated(signal_in, kernel, (1,), [(TAPS - 1, 0)], dimension_numbers=('NCH', 'OIH', 'NCH'), feature_group_count=D, precision=HIGHEST_PREC)[0].T
    gated_a = (queries * short_out).astype(jnp.bfloat16)
    partial_a = jnp.dot(gated_a, out_a, preferred_element_type=jnp.float32).astype(jnp.bfloat16)
    hidden = (tokens.astype(jnp.float32) + partial_a.astype(jnp.float32)).astype(jnp.bfloat16)
    normed_b = rms_scale(hidden, inv_rms_b, gain_b)
    projected_b = jnp.dot(normed_b, proj_b, preferred_element_type=jnp.float32)
    queries_b = projected_b[:, :D]
    signal = (projected_b[:, D:2 * D] * projected_b[:, 2 * D:]).astype(jnp.bfloat16)
    fft_size = 2 * TOKENS
    spectrum = jnp.fft.rfft(signal.astype(jnp.float32), n=fft_size, axis=0) * jnp.fft.rfft(long_filter(rates_b, residues_b), n=fft_size, axis=0)
    long_out = jnp.fft.irfft(spectrum, n=fft_size, axis=0)[:TOKENS].astype(jnp.bfloat16)
    long_out = lax.optimization_barrier(long_out)
    gated_b = (queries_b * long_out.astype(jnp.float32)).astype(jnp.bfloat16)
    partial_b = jnp.dot(gated_b, out_b, preferred_element_type=jnp.float32).astype(jnp.bfloat16)
    return (partial_a, partial_b)
```

```python
import functools

import jax
import jax.numpy as jnp
import numpy as np
from jax import lax
from jax.experimental import pallas as pl
from jax.experimental.pallas import tpu as pltpu
from jax.sharding import PartitionSpec as P

MESH = pl.DeviceIdType.MESH
F32 = jnp.float32
BF16 = jnp.bfloat16
SUB = 8
LANES = 128
QUAD = 4


def dft_tables(rows):
    freq = (np.arange(rows) + 0.5)[:, None]
    angle = freq * np.arange(rows)[None, :] * (np.pi / rows)
    cos, sin = np.cos(angle), np.sin(angle)
    sign = np.where(np.arange(rows) % 2 == 0, 1.0, -1.0)[:, None]
    own = np.concatenate([cos, sin], 0)
    behind = np.concatenate([sign * sin, -sign * cos], 0)
    back = own.T / rows
    return [jnp.asarray(t, F32).astype(BF16) for t in (own, behind, back)]


def dot(left, right):
    return jnp.dot(left, right, preferred_element_type=F32)


def split(value):
    high = value.astype(BF16)
    return high, (value - high.astype(F32)).astype(BF16)


def one_minus_exp(a):
    series = 1.0 - a / 9.0
    for k in (8.0, 7.0, 6.0, 5.0, 4.0, 3.0, 2.0):
        series = 1.0 - series * a / k
    return jnp.where(a < 0.5, a * series, 1.0 - jnp.exp(-a))


def column(row):
    rows = row.shape[1]
    eye = lax.broadcasted_iota(jnp.int32, (rows, rows), 0) == lax.broadcasted_iota(
        jnp.int32, (rows, rows), 1
    )
    return jnp.sum(jnp.where(eye, row, 0.0), axis=1, keepdims=True)


def scaled(tokens, scale, gain):
    return (tokens.astype(F32) * scale * gain).astype(BF16)


def spectral_product(data, filt):
    half = data.shape[0] // 2
    dc, ds, fc, fs = data[:half], data[half:], filt[:half], filt[half:]
    return jnp.concatenate([dc * fc - ds * fs, dc * fs + ds * fc], 0).astype(BF16)


def modes_over_rows(first, step, out_ref):
    rows, width = out_ref.shape
    for lane in range(0, width, LANES):
        cols = slice(lane, lane + LANES)
        term, ratio = first[:, :, cols], step[:, :, cols]
        for a in range(rows // SUB):
            out_ref[a * SUB : (a + 1) * SUB, cols] = jnp.sum(term, axis=0)
            if a + 1 < rows // SUB:
                term = term * ratio


def end_state(signal_ref, step, last):
    rows, width = signal_ref.shape
    parts = []
    for lane in range(0, width, LANES):
        cols = slice(lane, lane + LANES)
        ratio = step[:, :, cols]
        total = jnp.broadcast_to(signal_ref[0:SUB, cols][None], ratio.shape)
        for a in range(1, rows // SUB):
            total = total * ratio + signal_ref[a * SUB : (a + 1) * SUB, cols][None]
        parts.append(jnp.sum(total * last[:, :, cols], axis=1))
    return jnp.concatenate(parts, 1)


def hand_out(a_ref, b_ref, pa_ref, pb_ref, sem):
    copies = [
        pltpu.make_async_copy(a_ref, pa_ref, sem.at[0]),
        pltpu.make_async_copy(b_ref, pb_ref, sem.at[1]),
    ]
    for copy in copies:
        copy.start()
    for copy in copies:
        copy.wait()


def kernel(n, *refs):
    hbm = refs[:15]
    pa_ref, pb_ref = refs[15:17]
    vm = refs[17:32]
    (product_ref, rim_ref, filt_ref, signal_ref) = refs[32:36]
    (own_ref, mate_ref, pair_ref, front_ref, rear_ref, extra_ref) = refs[36:42]
    (load_sem, rim_send, rim_recv, mate_send, mate_recv) = refs[42:47]
    (near_send, far_send, front_recv, rear_recv, far_sem) = refs[47:]
    me = lax.axis_index("seq")
    rows, width = vm[0].shape
    modes = vm[9].shape[0]

    levels = n // QUAD
    level, place = me // QUAD, lax.rem(me, QUAD)
    base = level * QUAD
    mate = me + 1 - 2 * lax.rem(me, 2)
    speaker = (level == 0).astype(jnp.int32)
    front = place == speaker
    rear = place == 2
    speaks = jnp.logical_or(front, rear)
    greets = jnp.logical_or(place == 0, place == 2)
    seat = jnp.where(rear, 2, 0)
    barrier = pltpu.get_barrier_semaphore()

    def signal(sem, target):
        pl.semaphore_signal(sem, inc=1, device_id={"seq": target}, device_id_type=MESH)

    @pl.when(jnp.logical_and(place == 0, level > 0))
    def _():
        signal(barrier, me - 1)

    @pl.loop(1, QUAD)
    def _(i):
        signal(barrier, base + lax.rem(place + QUAD - i, QUAD))

    @pl.when(speaks)
    def _():
        @pl.loop(level + 1, levels)
        def _(i):
            signal(barrier, i * QUAD + seat)

    loads = [pltpu.make_async_copy(h, v, load_sem.at[i]) for i, (h, v) in enumerate(zip(hbm, vm))]
    order = (0, 1, 2, 3, 12, 4, 9, 10, 13, 14, 5, 6, 7, 8, 11)
    for i in order:
        loads[i].start()
    (tok, rms_a, gain_a, proj_a, taps, out_a) = vm[:6]
    (rms_b, gain_b, proj_b, rates_ref, resid_ref, out_b, own_f, rim_f, back_f) = vm[6:]

    @pl.when(me == 0)
    def _():
        rim_ref[...] = jnp.zeros_like(rim_ref)

    crossing = jnp.logical_and(place == QUAD - 1, level < levels - 1)
    arrivals = QUAD - 1 + jnp.where(greets, level, 0) + crossing.astype(jnp.int32)

    def greet():
        @pl.loop(0, level)
        def _(i):
            signal(far_sem, i * QUAD + jnp.where(rear, 2, (i == 0).astype(jnp.int32)))

    @pl.when(rear)
    def _():
        pl.semaphore_wait(barrier, arrivals)
        greet()

    for i in (0, 1, 2, 3):
        loads[i].wait()
    normed = scaled(tok[...], column(rms_a[...]), gain_a[...])
    projected = dot(normed, proj_a[...])
    queries = projected[:, :width]
    product = (projected[:, width : 2 * width] * projected[:, 2 * width :]).astype(BF16)
    product_ref[...] = product

    @pl.when(jnp.logical_not(rear))
    def _():
        pl.semaphore_wait(barrier, arrivals)

    rim_copy = pltpu.make_async_remote_copy(
        src_ref=product_ref,
        dst_ref=rim_ref,
        send_sem=rim_send,
        recv_sem=rim_recv,
        device_id={"seq": lax.rem(me + 1, n)},
        device_id_type=MESH,
    )

    @pl.when(me < n - 1)
    def _():
        rim_copy.start()

    @pl.when(place == 0)
    def _():
        greet()

    loads[12].wait()
    loads[4].wait()
    spectrum = dot(own_f[...], product)
    taps_spec = dot(own_f[...], taps[...])

    loads[9].wait()
    loads[10].wait()
    rates = rates_ref[...]
    length = float(n * rows)
    weights = resid_ref[...] * jnp.sqrt(
        one_minus_exp(2.0 * rates) / one_minus_exp(2.0 * rates * length)
    )
    rates3 = jnp.broadcast_to(rates[:, None, :], (modes, SUB, width))
    within = lax.broadcasted_iota(jnp.int32, (modes, SUB, width), 1).astype(F32)
    step = jnp.exp(-rates3 * float(SUB))
    lag = jnp.exp(-rates3 * within)
    last = jnp.exp(-rates3 * (SUB - 1.0 - within))
    read = jnp.exp(-rates3 * (within + 1.0))
    block = jnp.exp(-rates * float(rows))
    two_blocks = jnp.exp(-rates * float(2 * rows))
    four_blocks = jnp.exp(-rates * float(4 * rows))
    seated = jnp.exp(-rates * (place * rows).astype(F32))
    modes_over_rows(weights[:, None, :] * lag, step, filt_ref)
    high, low = split(filt_ref[...])
    long_spec = dot(own_f[...], high) + dot(own_f[...], low)
    for i in (13, 14, 5, 6, 7, 8, 11):
        loads[i].wait()
    scale_b = column(rms_b[...])

    @pl.when(me > 0)
    def _():
        rim_copy.wait_recv()

    carry = dot(rim_f[...], rim_ref[...])
    short_out = dot(back_f[...], spectral_product(spectrum + carry, taps_spec))
    gated_a = (queries * short_out).astype(BF16)
    partial_a = dot(gated_a, out_a[...]).astype(BF16)
    pa_ref[...] = partial_a
    hidden = (tok[...].astype(F32) + partial_a.astype(F32)).astype(BF16)
    normed_b = scaled(hidden, scale_b, gain_b[...])
    pair_b = dot(normed_b, proj_b[:, width:])
    signal_b = (pair_b[:, :width] * pair_b[:, width:]).astype(BF16)
    signal_ref[...] = signal_b.astype(F32)
    state = end_state(signal_ref, step, last)
    own_ref[...] = state

    mate_copy = pltpu.make_async_remote_copy(
        src_ref=own_ref,
        dst_ref=mate_ref,
        send_sem=mate_send,
        recv_sem=mate_recv,
        device_id={"seq": mate},
        device_id_type=MESH,
    )
    mate_copy.start()

    def front_copy(source, target, sem):
        return pltpu.make_async_remote_copy(
            src_ref=pair_ref,
            dst_ref=front_ref.at[source],
            send_sem=sem,
            recv_sem=front_recv.at[source],
            device_id={"seq": target},
            device_id_type=MESH,
        )

    def rear_copy(source, target, sem):
        return pltpu.make_async_remote_copy(
            src_ref=pair_ref,
            dst_ref=rear_ref.at[source],
            send_sem=sem,
            recv_sem=rear_recv.at[source],
            device_id={"seq": target},
            device_id_type=MESH,
        )

    mate_copy.wait_recv()
    early = lax.rem(place, 2) == 0
    pair_ref[...] = (
        jnp.where(early, state, mate_ref[...]) * block + jnp.where(early, mate_ref[...], state)
    ).astype(BF16)

    @pl.when(front)
    def _():
        for i in (1, 0):
            front_copy(level, base + 2 + i, near_send.at[i]).start()

    @pl.when(jnp.logical_and(speaks, level < levels - 1))
    def _():
        pl.semaphore_wait(far_sem, levels - 1 - level)

    def spread(copy, seats):
        for seat_there in seats:
            @pl.loop(level + 1, levels)
            def _(there):
                target = there * QUAD + seat_there
                copy(level, target, far_send.at[target]).start()

    @pl.when(front)
    def _():
        spread(front_copy, (1, 3, 0, 2))

    @pl.when(rear)
    def _():
        spread(rear_copy, (1, 0, 3, 2))

    queries_b = dot(normed_b, proj_b[:, :width])
    local = dot(back_f[...], spectral_product(dot(own_f[...], signal_b), long_spec))

    extra_ref[...] = jnp.where(place == 0, jnp.zeros_like(state), mate_ref[...])

    def gather(source, total):
        front_copy(source, mate, far_send.at[0]).wait_recv()
        pairs = front_ref[source].astype(F32) * two_blocks
        rear_copy(source, mate, far_send.at[0]).wait_recv()
        return total * four_blocks + (pairs + rear_ref[source].astype(F32))

    total = lax.fori_loop(0, level, gather, jnp.zeros((modes, width), F32))

    @pl.when(place >= 2)
    def _():
        front_copy(level, mate, far_send.at[0]).wait_recv()
        pairs = front_ref[level].astype(F32)
        extra_ref[...] = jnp.where(place == 2, pairs, pairs * block + extra_ref[...])

    total = total * seated + extra_ref[...]
    modes_over_rows((total * weights)[:, None, :] * read, step, filt_ref)
    long_out = (local + filt_ref[...]).astype(BF16)
    gated_b = (queries_b * long_out.astype(F32)).astype(BF16)
    pb_ref[...] = dot(gated_b, out_b[...]).astype(BF16)

    @pl.when(me < n - 1)
    def _():
        rim_copy.wait_send()

    mate_copy.wait_send()

    @pl.when(front)
    def _():
        for i in (0, 1):
            front_copy(level, base + 2 + i, near_send.at[i]).wait_send()

    @pl.when(speaks)
    def _():
        @pl.loop(base + QUAD, n)
        def _(target):
            front_copy(level, target, far_send.at[target]).wait_send()


def solution(mesh):
    n = mesh.shape["seq"]
    assert n % QUAD == 0

    def on_device(*args):
        rows, width = args[0].shape
        modes = args[9].shape[0]
        args = [a[None] if a.ndim == 1 else a for a in args] + dft_tables(rows)
        block = jax.ShapeDtypeStruct((rows, width), BF16)
        fast = pltpu.VMEM((rows, width), BF16)
        inside = pl.BlockSpec(memory_space=pltpu.VMEM)
        anywhere = pl.BlockSpec(memory_space=pl.ANY)
        results = pl.pallas_call(
            functools.partial(kernel, n),
            out_shape=(fast, fast),
            in_specs=[anywhere] * len(args),
            out_specs=(inside, inside),
            scratch_shapes=[pltpu.VMEM(a.shape, a.dtype) for a in args]
            + [
                pltpu.VMEM((rows, width), BF16),
                pltpu.VMEM((rows, width), BF16),
                pltpu.VMEM((rows, width), F32),
                pltpu.VMEM((rows, width), F32),
                pltpu.VMEM((modes, width), F32),
                pltpu.VMEM((modes, width), F32),
                pltpu.VMEM((modes, width), BF16),
                pltpu.VMEM((n // QUAD, modes, width), BF16),
                pltpu.VMEM((n // QUAD, modes, width), BF16),
                pltpu.VMEM((modes, width), F32),
                pltpu.SemaphoreType.DMA((len(args),)),
                pltpu.SemaphoreType.DMA,
                pltpu.SemaphoreType.DMA,
                pltpu.SemaphoreType.DMA,
                pltpu.SemaphoreType.DMA,
                pltpu.SemaphoreType.DMA((2,)),
                pltpu.SemaphoreType.DMA((n,)),
                pltpu.SemaphoreType.DMA((n // QUAD,)),
                pltpu.SemaphoreType.DMA((n // QUAD,)),
                pltpu.SemaphoreType.REGULAR,
            ],
            compiler_params=pltpu.CompilerParams(collective_id=0, has_side_effects=True),
        )(*args)
        return pl.pallas_call(
            hand_out,
            out_shape=(block, block),
            in_specs=[inside] * 2,
            out_specs=(anywhere, anywhere),
            scratch_shapes=[pltpu.SemaphoreType.DMA((2,))],
        )(*[pltpu.with_memory_space_constraint(r, pltpu.VMEM) for r in results])

    shard = P(("groups", "seq"))
    wide = P(("groups", "seq"), None)
    placed = (wide, shard, P(), P(), P(), P(), shard, P(), P(), P(), P(), P())
    return jax.shard_map(
        on_device, mesh=mesh, in_specs=placed, out_specs=(wide, wide), check_vma=False
    )
```

```python
import functools

import jax
import jax.numpy as jnp
import numpy as np
from jax import lax
from jax.experimental import pallas as pl
from jax.experimental.pallas import tpu as pltpu
from jax.sharding import PartitionSpec as P

MESH = pl.DeviceIdType.MESH
F32 = jnp.float32
BF16 = jnp.bfloat16
SUB = 8
LANES = 128
QUAD = 4


def dft_tables(rows):
    freq = (np.arange(rows) + 0.5)[:, None]
    angle = freq * np.arange(rows)[None, :] * (np.pi / rows)
    cos, sin = np.cos(angle), np.sin(angle)
    sign = np.where(np.arange(rows) % 2 == 0, 1.0, -1.0)[:, None]
    own = np.concatenate([cos, sin], 0)
    behind = np.concatenate([sign * sin, -sign * cos], 0)
    back = own.T / rows
    return [jnp.asarray(t, F32).astype(BF16) for t in (own, behind, back)]


def dot(left, right):
    return jnp.dot(left, right, preferred_element_type=F32)


def split(value):
    high = value.astype(BF16)
    return high, (value - high.astype(F32)).astype(BF16)


def one_minus_exp(a):
    series = 1.0 - a / 9.0
    for k in (8.0, 7.0, 6.0, 5.0, 4.0, 3.0, 2.0):
        series = 1.0 - series * a / k
    return jnp.where(a < 0.5, a * series, 1.0 - jnp.exp(-a))


def column(row):
    rows = row.shape[1]
    eye = lax.broadcasted_iota(jnp.int32, (rows, rows), 0) == lax.broadcasted_iota(
        jnp.int32, (rows, rows), 1
    )
    return jnp.sum(jnp.where(eye, row, 0.0), axis=1, keepdims=True)


def scaled(tokens, scale, gain):
    return (tokens.astype(F32) * scale * gain).astype(BF16)


def spectral_product(data, filt):
    half = data.shape[0] // 2
    dc, ds, fc, fs = data[:half], data[half:], filt[:half], filt[half:]
    return jnp.concatenate([dc * fc - ds * fs, dc * fs + ds * fc], 0).astype(BF16)


def modes_over_rows(first, step, out_ref):
    rows, width = out_ref.shape
    for lane in range(0, width, LANES):
        cols = slice(lane, lane + LANES)
        term, ratio = first[:, :, cols], step[:, :, cols]
        for a in range(rows // SUB):
            out_ref[a * SUB : (a + 1) * SUB, cols] = jnp.sum(term, axis=0)
            if a + 1 < rows // SUB:
                term = term * ratio


def sublane_sums(parts):
    row = lax.broadcasted_iota(jnp.int32, parts[0].shape, 0)
    high = row >= 4
    parts = [
        jnp.where(high, b, a) + pltpu.roll(jnp.where(high, a, b), 4, 0)
        for a, b in zip(parts[:4], parts[4:])
    ]
    for shift in (2, 1):
        odd = lax.rem(row // shift, 2) == 1
        count = len(parts) // 2
        parts = [
            jnp.where(odd, b + pltpu.roll(b, shift, 0), a + pltpu.roll(a, SUB - shift, 0))
            for a, b in zip(parts[:count], parts[count:])
        ]
    return parts[0]


def end_state(signal, step, last):
    rows, width = signal.shape
    modes = step.shape[0]
    columns = []
    for lane in range(0, width, LANES):
        cols = slice(lane, lane + LANES)
        tiles = [signal[r : r + SUB, cols] for r in range(0, rows, SUB)]
        groups = []
        for first in range(0, modes, SUB):
            parts = []
            for m in range(first, first + SUB):
                ratio, total = step[m, :, cols], tiles[0]
                for tile in tiles[1:]:
                    total = total * ratio + tile
                parts.append(total * last[m, :, cols])
            groups.append(sublane_sums(parts))
        columns.append(jnp.concatenate(groups, 0))
    return jnp.concatenate(columns, 1)


def hand_out(a_ref, b_ref, pa_ref, pb_ref, sem):
    copies = [
        pltpu.make_async_copy(a_ref, pa_ref, sem.at[0]),
        pltpu.make_async_copy(b_ref, pb_ref, sem.at[1]),
    ]
    for copy in copies:
        copy.start()
    for copy in copies:
        copy.wait()


def kernel(n, *refs):
    hbm = refs[:15]
    pa_ref, pb_ref = refs[15:17]
    vm = refs[17:32]
    (tail_ref, rim_ref, filt_ref, signal_ref) = refs[32:36]
    (own_ref, mate_ref, pair_ref, front_ref, rear_ref, extra_ref) = refs[36:42]
    (load_sem, rim_send, rim_recv, mate_send, mate_recv) = refs[42:47]
    (near_send, far_send, front_recv, rear_recv, far_sem) = refs[47:]
    me = lax.axis_index("seq")
    rows, width = vm[0].shape
    modes = vm[9].shape[0]

    levels = n // QUAD
    level, place = me // QUAD, lax.rem(me, QUAD)
    base = level * QUAD
    mate = me + 1 - 2 * lax.rem(me, 2)
    speaker = (level == 0).astype(jnp.int32)
    front = place == speaker
    rear = place == 2
    speaks = jnp.logical_or(front, rear)
    barrier = pltpu.get_barrier_semaphore()

    def signal(sem, target):
        pl.semaphore_signal(sem, inc=1, device_id={"seq": target}, device_id_type=MESH)

    @pl.when(jnp.logical_and(place == 0, level > 0))
    def _():
        signal(barrier, me - 1)

    @pl.loop(1, QUAD)
    def _(i):
        signal(barrier, base + lax.rem(place + QUAD - i, QUAD))

    @pl.when(speaks)
    def _():
        @pl.loop(level + 1, levels)
        def _(i):
            signal(barrier, i * QUAD + 2)

    loads = [pltpu.make_async_copy(h, v, load_sem.at[i]) for i, (h, v) in enumerate(zip(hbm, vm))]
    order = (0, 1, 2, 3, 12, 4, 13, 14, 9, 10, 5, 6, 7, 8, 11)
    for i in order:
        loads[i].start()
    (tok, rms_a, gain_a, proj_a, taps, out_a) = vm[:6]
    (rms_b, gain_b, proj_b, rates_ref, resid_ref, out_b, own_f, rim_f, back_f) = vm[6:]

    @pl.when(me == 0)
    def _():
        rim_ref[...] = jnp.zeros_like(rim_ref)

    crossing = jnp.logical_and(place == QUAD - 1, level < levels - 1)

    @pl.when(rear)
    def _():
        pl.semaphore_wait(barrier, QUAD - 1 + 2 * level)

        @pl.loop(0, level)
        def _(i):
            signal(far_sem, i * QUAD + (i == 0).astype(jnp.int32))
            signal(far_sem, i * QUAD + 2)

    for i in (0, 1, 2, 3):
        loads[i].wait()
    normed = scaled(tok[...], column(rms_a[...]), gain_a[...])
    projected = dot(normed, proj_a[...])
    queries = projected[:, :width]
    product = (projected[:, width : 2 * width] * projected[:, 2 * width :]).astype(BF16)
    for i in (12, 4, 13, 14):
        loads[i].wait()
    taps_spec = dot(own_f[...], taps[...])
    tail_ref[...] = dot(
        back_f[...], spectral_product(dot(rim_f[...], product), taps_spec)
    ).astype(BF16)

    @pl.when(jnp.logical_not(rear))
    def _():
        pl.semaphore_wait(barrier, QUAD - 1 + crossing.astype(jnp.int32))

    rim_copy = pltpu.make_async_remote_copy(
        src_ref=tail_ref,
        dst_ref=rim_ref,
        send_sem=rim_send,
        recv_sem=rim_recv,
        device_id={"seq": lax.rem(me + 1, n)},
        device_id_type=MESH,
    )

    @pl.when(me < n - 1)
    def _():
        rim_copy.start()

    short_own = dot(back_f[...], spectral_product(dot(own_f[...], product), taps_spec))

    loads[9].wait()
    loads[10].wait()
    rates = rates_ref[...]
    length = float(n * rows)
    rates3 = jnp.broadcast_to(rates[:, None, :], (modes, SUB, width))
    within = lax.broadcasted_iota(jnp.int32, (modes, SUB, width), 1).astype(F32)
    step = jnp.exp(-rates3 * float(SUB))
    last = jnp.exp(-rates3 * (SUB - 1.0 - within))
    block = jnp.exp(-rates * float(rows))
    for i in (5, 6, 7, 8, 11):
        loads[i].wait()
    scale_b = column(rms_b[...])
    base_b = dot(scaled(tok[...], scale_b, gain_b[...]), proj_b[...])
    high, low = split(out_a[...].astype(F32) * gain_b[...])
    through = (dot(high, proj_b[...]) + dot(low, proj_b[...])).astype(BF16)

    @pl.when(me > 0)
    def _():
        rim_copy.wait_recv()

    short_out = short_own + rim_ref[...].astype(F32)
    gated_a = (queries * short_out).astype(BF16)
    pair_b = base_b[:, width:] + scale_b * dot(gated_a, through[:, width:])
    signal_b = (pair_b[:, :width] * pair_b[:, width:]).astype(BF16)
    signal_ref[...] = signal_b.astype(F32)
    state = end_state(signal_ref, step, last)
    own_ref[...] = state

    mate_copy = pltpu.make_async_remote_copy(
        src_ref=own_ref,
        dst_ref=mate_ref,
        send_sem=mate_send,
        recv_sem=mate_recv,
        device_id={"seq": mate},
        device_id_type=MESH,
    )
    mate_copy.start()

    def front_copy(source, target, sem):
        return pltpu.make_async_remote_copy(
            src_ref=pair_ref,
            dst_ref=front_ref.at[source],
            send_sem=sem,
            recv_sem=front_recv.at[source],
            device_id={"seq": target},
            device_id_type=MESH,
        )

    def rear_copy(source, target, sem):
        return pltpu.make_async_remote_copy(
            src_ref=pair_ref,
            dst_ref=rear_ref.at[source],
            send_sem=sem,
            recv_sem=rear_recv.at[source],
            device_id={"seq": target},
            device_id_type=MESH,
        )

    mate_copy.wait_recv()
    early = lax.rem(place, 2) == 0
    pair_ref[...] = (
        jnp.where(early, state, mate_ref[...]) * block + jnp.where(early, mate_ref[...], state)
    ).astype(BF16)

    @pl.when(front)
    def _():
        for i in (1, 0):
            front_copy(level, base + 2 + i, near_send.at[i]).start()

    @pl.when(jnp.logical_and(speaks, level < levels - 1))
    def _():
        pl.semaphore_wait(far_sem, levels - 1 - level)

    def spread(copy, seats):
        for seat_there, outward in seats:
            @pl.loop(0, levels - 1 - level)
            def _(i):
                there = level + 1 + i if outward else levels - 1 - i
                target = there * QUAD + seat_there
                copy(level, target, far_send.at[target]).start()

    @pl.when(front)
    def _():
        spread(front_copy, ((1, False), (0, False), (3, False), (2, False)))

    @pl.when(rear)
    def _():
        spread(rear_copy, ((1, False), (0, True), (3, False), (2, False)))

    pa_ref[...] = dot(gated_a, out_a[...]).astype(BF16)
    queries_b = base_b[:, :width] + scale_b * dot(gated_a, through[:, :width])
    length = float(n * rows)
    weights = resid_ref[...] * jnp.sqrt(
        one_minus_exp(2.0 * rates) / one_minus_exp(2.0 * rates * length)
    )
    modes_over_rows(weights[:, None, :] * jnp.exp(-rates3 * within), step, filt_ref)
    high, low = split(filt_ref[...])
    long_spec = dot(own_f[...], high) + dot(own_f[...], low)
    read = jnp.exp(-rates3 * (within + 1.0))
    two_blocks = jnp.exp(-rates * float(2 * rows))
    four_blocks = jnp.exp(-rates * float(4 * rows))
    seated = jnp.exp(-rates * (place * rows).astype(F32))
    local = dot(back_f[...], spectral_product(dot(own_f[...], signal_b), long_spec))

    extra_ref[...] = jnp.where(place == 0, jnp.zeros_like(state), mate_ref[...])

    def gather(source, total):
        front_copy(source, mate, far_send.at[0]).wait_recv()
        pairs = front_ref[source].astype(F32) * two_blocks
        rear_copy(source, mate, far_send.at[0]).wait_recv()
        return total * four_blocks + (pairs + rear_ref[source].astype(F32))

    total = lax.fori_loop(0, level, gather, jnp.zeros((modes, width), F32))

    @pl.when(place >= 2)
    def _():
        front_copy(level, mate, far_send.at[0]).wait_recv()
        pairs = front_ref[level].astype(F32)
        extra_ref[...] = jnp.where(place == 2, pairs, pairs * block + extra_ref[...])

    total = total * seated + extra_ref[...]
    modes_over_rows((total * weights)[:, None, :] * read, step, filt_ref)
    long_out = (local + filt_ref[...]).astype(BF16)
    gated_b = (queries_b * long_out.astype(F32)).astype(BF16)
    pb_ref[...] = dot(gated_b, out_b[...]).astype(BF16)

    @pl.when(me < n - 1)
    def _():
        rim_copy.wait_send()

    mate_copy.wait_send()

    @pl.when(front)
    def _():
        for i in (0, 1):
            front_copy(level, base + 2 + i, near_send.at[i]).wait_send()

    @pl.when(speaks)
    def _():
        @pl.loop(base + QUAD, n)
        def _(target):
            front_copy(level, target, far_send.at[target]).wait_send()


def solution(mesh):
    n = mesh.shape["seq"]
    assert n % QUAD == 0

    def on_device(*args):
        rows, width = args[0].shape
        modes = args[9].shape[0]
        args = [a[None] if a.ndim == 1 else a for a in args] + dft_tables(rows)
        block = jax.ShapeDtypeStruct((rows, width), BF16)
        fast = pltpu.VMEM((rows, width), BF16)
        inside = pl.BlockSpec(memory_space=pltpu.VMEM)
        anywhere = pl.BlockSpec(memory_space=pl.ANY)
        results = pl.pallas_call(
            functools.partial(kernel, n),
            out_shape=(fast, fast),
            in_specs=[anywhere] * len(args),
            out_specs=(inside, inside),
            scratch_shapes=[pltpu.VMEM(a.shape, a.dtype) for a in args]
            + [
                pltpu.VMEM((rows, width), BF16),
                pltpu.VMEM((rows, width), BF16),
                pltpu.VMEM((rows, width), F32),
                pltpu.VMEM((rows, width), F32),
                pltpu.VMEM((modes, width), F32),
                pltpu.VMEM((modes, width), F32),
                pltpu.VMEM((modes, width), BF16),
                pltpu.VMEM((n // QUAD, modes, width), BF16),
                pltpu.VMEM((n // QUAD, modes, width), BF16),
                pltpu.VMEM((modes, width), F32),
                pltpu.SemaphoreType.DMA((len(args),)),
                pltpu.SemaphoreType.DMA,
                pltpu.SemaphoreType.DMA,
                pltpu.SemaphoreType.DMA,
                pltpu.SemaphoreType.DMA,
                pltpu.SemaphoreType.DMA((2,)),
                pltpu.SemaphoreType.DMA((n,)),
                pltpu.SemaphoreType.DMA((n // QUAD,)),
                pltpu.SemaphoreType.DMA((n // QUAD,)),
                pltpu.SemaphoreType.REGULAR,
            ],
            compiler_params=pltpu.CompilerParams(collective_id=0, has_side_effects=True),
        )(*args)
        return pl.pallas_call(
            hand_out,
            out_shape=(block, block),
            in_specs=[inside] * 2,
            out_specs=(anywhere, anywhere),
            scratch_shapes=[pltpu.SemaphoreType.DMA((2,))],
        )(*[pltpu.with_memory_space_constraint(r, pltpu.VMEM) for r in results])

    shard = P(("groups", "seq"))
    wide = P(("groups", "seq"), None)
    placed = (wide, shard, P(), P(), P(), P(), shard, P(), P(), P(), P(), P())
    return jax.shard_map(
        on_device, mesh=mesh, in_specs=placed, out_specs=(wide, wide), check_vma=False
    )
```

```python
import functools

import jax
import jax.numpy as jnp
import numpy as np
from jax import lax
from jax.experimental import pallas as pl
from jax.experimental.pallas import tpu as pltpu
from jax.sharding import PartitionSpec as P

MESH = pl.DeviceIdType.MESH
F32 = jnp.float32
BF16 = jnp.bfloat16
SUB = 8
LANES = 128
QUAD = 4
PIECES = 2


def dft_tables(rows):
    freq = (np.arange(rows) + 0.5)[:, None]
    angle = freq * np.arange(rows)[None, :] * (np.pi / rows)
    cos, sin = np.cos(angle), np.sin(angle)
    sign = np.where(np.arange(rows) % 2 == 0, 1.0, -1.0)[:, None]
    own = np.concatenate([cos, sin], 0)
    behind = np.concatenate([sign * sin, -sign * cos], 0)
    back = own.T / rows
    return [jnp.asarray(t, F32).astype(BF16) for t in (own, behind, back)]


def dot(left, right):
    return jnp.dot(left, right, preferred_element_type=F32)


def split(value):
    high = value.astype(BF16)
    return high, (value - high.astype(F32)).astype(BF16)


def one_minus_exp(a):
    series = 1.0 - a / 9.0
    for k in (8.0, 7.0, 6.0, 5.0, 4.0, 3.0, 2.0):
        series = 1.0 - series * a / k
    return jnp.where(a < 0.5, a * series, 1.0 - jnp.exp(-a))


def column(row):
    rows = row.shape[1]
    eye = lax.broadcasted_iota(jnp.int32, (rows, rows), 0) == lax.broadcasted_iota(
        jnp.int32, (rows, rows), 1
    )
    return jnp.sum(jnp.where(eye, row, 0.0), axis=1, keepdims=True)


def scaled(tokens, scale, gain):
    return (tokens.astype(F32) * scale * gain).astype(BF16)


def spectral_product(data, filt):
    half = data.shape[0] // 2
    dc, ds, fc, fs = data[:half], data[half:], filt[:half], filt[half:]
    return jnp.concatenate([dc * fc - ds * fs, dc * fs + ds * fc], 0).astype(BF16)


def modes_over_rows(first, step, out_ref):
    rows, width = out_ref.shape
    for lane in range(0, width, LANES):
        cols = slice(lane, lane + LANES)
        term, ratio = first[:, :, cols], step[:, :, cols]
        for a in range(rows // SUB):
            out_ref[a * SUB : (a + 1) * SUB, cols] = jnp.sum(term, axis=0)
            if a + 1 < rows // SUB:
                term = term * ratio


def sublane_sums(parts):
    row = lax.broadcasted_iota(jnp.int32, parts[0].shape, 0)
    high = row >= 4
    parts = [
        jnp.where(high, b, a) + pltpu.roll(jnp.where(high, a, b), 4, 0)
        for a, b in zip(parts[:4], parts[4:])
    ]
    for shift in (2, 1):
        odd = lax.rem(row // shift, 2) == 1
        count = len(parts) // 2
        parts = [
            jnp.where(odd, b + pltpu.roll(b, shift, 0), a + pltpu.roll(a, SUB - shift, 0))
            for a, b in zip(parts[:count], parts[count:])
        ]
    return parts[0]


def end_totals(totals, signal, step):
    rows, width = signal.shape
    modes = step.shape[0]
    sums = {}
    for lane in range(0, width, LANES):
        cols = slice(lane, lane + LANES)
        tiles = [signal[r : r + SUB, cols] for r in range(0, rows, SUB)]
        for m in range(modes):
            total, rest = (tiles[0], tiles[1:]) if totals is None else (totals[lane, m], tiles)
            for tile in rest:
                total = total * step[m, :, cols] + tile
            sums[lane, m] = total
    return sums


def end_state(totals, last):
    modes, _, width = last.shape
    columns = []
    for lane in range(0, width, LANES):
        parts = [totals[lane, m] * last[m, :, lane : lane + LANES] for m in range(modes)]
        columns.append(
            jnp.concatenate([sublane_sums(parts[m : m + SUB]) for m in range(0, modes, SUB)], 0)
        )
    return jnp.concatenate(columns, 1)


def size(ref):
    return int(np.prod(ref.shape)) * ref.dtype.itemsize


def settle(span_ref, sem, total):
    part = span_ref.at[pl.ds(0, total // (LANES * 4))]
    pltpu.make_async_copy(part, part, sem).wait()


def hand_out(a_ref, b_ref, pa_ref, pb_ref, span_ref, sem):
    copies = [
        pltpu.make_async_copy(a_ref, pa_ref, sem),
        pltpu.make_async_copy(b_ref, pb_ref, sem),
    ]
    for copy in copies:
        copy.start()
    settle(span_ref, sem, size(a_ref) + size(b_ref))


def kernel(n, *refs):
    hbm = refs[:15]
    pa_ref, pb_ref = refs[15:17]
    vm = refs[17:32]
    (tail_ref, rim_ref, filt_ref, signal_ref, gated_ref) = refs[32:37]
    (own_ref, mate_ref, pair_ref, front_ref, rear_ref, extra_ref, span_ref) = refs[37:44]
    (load_sem, send_sem, rim_recv, mate_recv, far_recv, far_sem) = refs[44:]
    rows, width = vm[0].shape
    modes = vm[9].shape[0]

    groups = ((1, 2, 0), (3,), (12, 4, 13, 14), (15, 9, 10, 5, 6, 7, 8, 11))
    pairs_of = dict(enumerate(zip(hbm, vm)))
    keys = (slice(None), pl.ds(width, 2 * width))
    queries_only = (slice(None), pl.ds(0, width))
    pairs_of[3] = (hbm[3].at[keys], vm[3].at[keys])
    pairs_of[15] = (hbm[3].at[queries_only], vm[3].at[queries_only])
    loads = [
        [pltpu.make_async_copy(*pairs_of[i], load_sem.at[g]) for i in group]
        for g, group in enumerate(groups)
    ]

    def start(*which):
        for g in which:
            for load in loads[g]:
                load.start()

    def arrive(g):
        settle(span_ref, load_sem.at[g], sum(size(pairs_of[i][1]) for i in groups[g]))

    start(0, 1)
    me = lax.axis_index("seq")

    levels = n // QUAD
    level, place = me // QUAD, lax.rem(me, QUAD)
    base = level * QUAD
    mate = me + 1 - 2 * lax.rem(me, 2)
    speaker = (level == 0).astype(jnp.int32)
    front = place == speaker
    rear = place == 2
    speaks = jnp.logical_or(front, rear)
    barrier = pltpu.get_barrier_semaphore()

    def signal(sem, target):
        pl.semaphore_signal(sem, inc=1, device_id={"seq": target}, device_id_type=MESH)

    @pl.when(jnp.logical_and(place == 0, level > 0))
    def _():
        signal(barrier, me - 1)

    @pl.loop(1, QUAD)
    def _(i):
        signal(barrier, base + lax.rem(place + QUAD - i, QUAD))

    @pl.when(speaks)
    def _():
        @pl.loop(level + 1, levels)
        def _(i):
            signal(barrier, i * QUAD + 2)

    start(2, 3)
    (tok, rms_a, gain_a, proj_a, taps, out_a) = vm[:6]
    (rms_b, gain_b, proj_b, rates_ref, resid_ref, out_b, own_f, rim_f, back_f) = vm[6:]

    piece = rows // PIECES
    pieces = [pl.ds(p * piece, piece) for p in range(PIECES)]

    @pl.when(me == 0)
    def _():
        gated_ref[...] = jnp.zeros_like(gated_ref)
        for i, p in enumerate(pieces):
            pltpu.make_async_copy(gated_ref.at[p], rim_ref.at[p], rim_recv.at[i]).start()

    crossing = jnp.logical_and(place == QUAD - 1, level < levels - 1)

    @pl.when(rear)
    def _():
        pl.semaphore_wait(barrier, QUAD - 1 + 2 * level)

        @pl.loop(0, level)
        def _(i):
            signal(far_sem, i * QUAD + (i == 0).astype(jnp.int32))
            signal(far_sem, i * QUAD + 2)

    arrive(0)
    normed = scaled(tok[...], column(rms_a[...]), gain_a[...])
    arrive(1)
    pair_a = dot(normed, proj_a[:, width:])
    product = (pair_a[:, :width] * pair_a[:, width:]).astype(BF16)
    arrive(2)
    taps_spec = dot(own_f[...], taps[...])
    tail_ref[...] = dot(
        back_f[...], spectral_product(dot(rim_f[...], product), taps_spec)
    ).astype(BF16)

    @pl.when(jnp.logical_not(rear))
    def _():
        pl.semaphore_wait(barrier, QUAD - 1 + crossing.astype(jnp.int32))

    rim_copies = [
        pltpu.make_async_remote_copy(
            src_ref=tail_ref.at[p],
            dst_ref=rim_ref.at[p],
            send_sem=send_sem,
            recv_sem=rim_recv.at[i],
            device_id={"seq": lax.rem(me + 1, n)},
            device_id_type=MESH,
        )
        for i, p in enumerate(pieces)
    ]

    @pl.when(me < n - 1)
    def _():
        for copy in rim_copies:
            copy.start()

    arrive(3)
    queries = dot(normed, proj_a[:, :width])
    short_own = dot(back_f[...], spectral_product(dot(own_f[...], product), taps_spec))

    rates = rates_ref[...]
    length = float(n * rows)
    rates3 = jnp.broadcast_to(rates[:, None, :], (modes, SUB, width))
    within = lax.broadcasted_iota(jnp.int32, (modes, SUB, width), 1).astype(F32)
    step = jnp.exp(-rates3 * float(SUB))
    last = jnp.exp(-rates3 * (SUB - 1.0 - within))
    block = jnp.exp(-rates * float(rows))
    scale_b = column(rms_b[...])
    base_b = dot(scaled(tok[...], scale_b, gain_b[...]), proj_b[...])
    high, low = split(out_a[...].astype(F32) * gain_b[...])
    through = (dot(high, proj_b[...]) + dot(low, proj_b[...])).astype(BF16)

    totals = None
    for i, p in enumerate(pieces):
        rim_copies[i].wait_recv()
        span = slice(i * piece, (i + 1) * piece)
        gated = (queries[span] * (short_own[span] + rim_ref[p].astype(F32))).astype(BF16)
        gated_ref[p] = gated
        pair_b = base_b[span, width:] + scale_b[span] * dot(gated, through[:, width:])
        signal = (pair_b[:, :width] * pair_b[:, width:]).astype(BF16)
        signal_ref[p] = signal
        totals = end_totals(totals, signal.astype(F32), step)
    state = end_state(totals, last)
    own_ref[...] = state

    mate_copy = pltpu.make_async_remote_copy(
        src_ref=own_ref,
        dst_ref=mate_ref,
        send_sem=send_sem,
        recv_sem=mate_recv,
        device_id={"seq": mate},
        device_id_type=MESH,
    )
    mate_copy.start()

    def far_copy(slots, target, there):
        return pltpu.make_async_remote_copy(
            src_ref=pair_ref,
            dst_ref=slots.at[level],
            send_sem=send_sem,
            recv_sem=far_recv.at[(there - level <= 1).astype(jnp.int32)],
            device_id={"seq": target},
            device_id_type=MESH,
        )

    mate_copy.wait_recv()
    early = lax.rem(place, 2) == 0
    pair_ref[...] = (
        jnp.where(early, state, mate_ref[...]) * block + jnp.where(early, mate_ref[...], state)
    ).astype(BF16)

    @pl.when(front)
    def _():
        for i in (1, 0):
            far_copy(front_ref, base + 2 + i, level).start()

    @pl.when(jnp.logical_and(speaks, level < levels - 1))
    def _():
        pl.semaphore_wait(far_sem, levels - 1 - level)

    def spread(slots, seats):
        for seat_there, outward in seats:
            @pl.loop(0, levels - 1 - level)
            def _(i):
                there = level + 1 + i if outward else levels - 1 - i
                target = there * QUAD + seat_there
                far_copy(slots, target, there).start()

    @pl.when(front)
    def _():
        spread(front_ref, ((1, False), (0, False), (3, False), (2, False)))

    @pl.when(rear)
    def _():
        spread(rear_ref, ((1, False), (0, True), (3, False), (2, False)))

    pa_ref[...] = dot(gated_ref[...], out_a[...]).astype(BF16)
    queries_b = base_b[:, :width] + scale_b * dot(gated_ref[...], through[:, :width])
    length = float(n * rows)
    weights = resid_ref[...] * jnp.sqrt(
        one_minus_exp(2.0 * rates) / one_minus_exp(2.0 * rates * length)
    )
    modes_over_rows(weights[:, None, :] * jnp.exp(-rates3 * within), step, filt_ref)
    high, low = split(filt_ref[...])
    long_spec = dot(own_f[...], high) + dot(own_f[...], low)
    read = jnp.exp(-rates3 * (within + 1.0))
    two_blocks = jnp.exp(-rates * float(2 * rows))
    four_blocks = jnp.exp(-rates * float(4 * rows))
    seated = jnp.exp(-rates * (place * rows).astype(F32))
    local = dot(back_f[...], spectral_product(dot(own_f[...], signal_ref[...]), long_spec))

    extra_ref[...] = jnp.where(place == 0, jnp.zeros_like(state), mate_ref[...])

    always = size(rim_ref) + size(own_ref)
    letter = size(pair_ref)

    @pl.when(jnp.logical_and(jnp.logical_not(speaks), me < n - 1))
    def _():
        settle(span_ref, send_sem, always)

    @pl.when(me == n - 1)
    def _():
        settle(span_ref, send_sem, size(own_ref))

    for there in range(levels):
        rest = (levels - 1 - there) * QUAD

        @pl.when(jnp.logical_and(front, level == there))
        def _():
            settle(span_ref, send_sem, always + (rest + 2) * letter)

        @pl.when(jnp.logical_and(rear, level == there))
        def _():
            settle(span_ref, send_sem, always + rest * letter)

    def gather(source, total):
        pairs = front_ref[source].astype(F32) * two_blocks
        return total * four_blocks + (pairs + rear_ref[source].astype(F32))

    older = jnp.maximum(level - 1, 0)
    for there in range(2, levels):

        @pl.when(level == there)
        def _():
            settle(span_ref, far_recv.at[0], 2 * (there - 1) * letter)

    total = lax.fori_loop(0, older, gather, jnp.zeros((modes, width), F32))
    back = place >= 2

    @pl.when(jnp.logical_and(level > 0, jnp.logical_not(back)))
    def _():
        settle(span_ref, far_recv.at[1], 2 * letter)

    @pl.when(jnp.logical_and(level > 0, back))
    def _():
        settle(span_ref, far_recv.at[1], 3 * letter)

    @pl.when(jnp.logical_and(level == 0, back))
    def _():
        settle(span_ref, far_recv.at[1], letter)

    total = lax.fori_loop(older, level, gather, total)

    @pl.when(place >= 2)
    def _():
        pairs = front_ref[level].astype(F32)
        extra_ref[...] = jnp.where(place == 2, pairs, pairs * block + extra_ref[...])

    total = total * seated + extra_ref[...]
    modes_over_rows((total * weights)[:, None, :] * read, step, filt_ref)
    long_out = (local + filt_ref[...]).astype(BF16)
    gated_b = (queries_b * long_out.astype(F32)).astype(BF16)
    pb_ref[...] = dot(gated_b, out_b[...]).astype(BF16)


def solution(mesh):
    n = mesh.shape["seq"]
    assert n % QUAD == 0

    def on_device(*args):
        rows, width = args[0].shape
        modes = args[9].shape[0]
        args = [a[None] if a.ndim == 1 else a for a in args] + dft_tables(rows)
        block = jax.ShapeDtypeStruct((rows, width), BF16)
        span = sum(size(a) for a in args) + (n + 8) * modes * width * 2
        fast = pltpu.VMEM((rows, width), BF16)
        inside = pl.BlockSpec(memory_space=pltpu.VMEM)
        anywhere = pl.BlockSpec(memory_space=pl.ANY)
        results = pl.pallas_call(
            functools.partial(kernel, n),
            out_shape=(fast, fast),
            in_specs=[anywhere] * len(args),
            out_specs=(inside, inside),
            scratch_shapes=[pltpu.VMEM(a.shape, a.dtype) for a in args]
            + [
                pltpu.VMEM((rows, width), BF16),
                pltpu.VMEM((rows, width), BF16),
                pltpu.VMEM((rows, width), F32),
                pltpu.VMEM((rows, width), BF16),
                pltpu.VMEM((rows, width), BF16),
                pltpu.VMEM((modes, width), F32),
                pltpu.VMEM((modes, width), F32),
                pltpu.VMEM((modes, width), BF16),
                pltpu.VMEM((n // QUAD, modes, width), BF16),
                pltpu.VMEM((n // QUAD, modes, width), BF16),
                pltpu.VMEM((modes, width), F32),
                pltpu.VMEM((span // (4 * LANES), 1, LANES), F32),
                pltpu.SemaphoreType.DMA((4,)),
                pltpu.SemaphoreType.DMA,
                pltpu.SemaphoreType.DMA((PIECES,)),
                pltpu.SemaphoreType.DMA,
                pltpu.SemaphoreType.DMA((2,)),
                pltpu.SemaphoreType.REGULAR,
            ],
            compiler_params=pltpu.CompilerParams(collective_id=0, has_side_effects=True),
        )(*args)
        return pl.pallas_call(
            hand_out,
            out_shape=(block, block),
            in_specs=[inside] * 2,
            out_specs=(anywhere, anywhere),
            scratch_shapes=[
                pltpu.VMEM((2 * rows * width * 2 // (4 * LANES), 1, LANES), F32),
                pltpu.SemaphoreType.DMA,
            ],
        )(*[pltpu.with_memory_space_constraint(r, pltpu.VMEM) for r in results])

    shard = P(("groups", "seq"))
    wide = P(("groups", "seq"), None)
    placed = (wide, shard, P(), P(), P(), P(), shard, P(), P(), P(), P(), P())
    return jax.shard_map(
        on_device, mesh=mesh, in_specs=placed, out_specs=(wide, wide), check_vma=False
    )
```

```python
import functools

import jax
import jax.numpy as jnp
import numpy as np
from jax import lax
from jax.experimental import pallas as pl
from jax.experimental.pallas import tpu as pltpu
from jax.sharding import PartitionSpec as P

MESH = pl.DeviceIdType.MESH
F32 = jnp.float32
BF16 = jnp.bfloat16
SUB = 8
LANES = 128
QUAD = 4
PIECES = 2
FRONT_PLAN = [(None, 0), (3, 0), (1, 0), (2, 0), (0, 0), (None, 1), (3, 1), (1, 1), (2, 1), (0, 1)]
REAR_PLAN = [(None, 0), (None, 1), (1, 1), (1, 0), (0, 0), (0, 1), (3, 1), (3, 0), (2, 1), (2, 0)]


def dft_tables(rows):
    freq = (np.arange(rows) + 0.5)[:, None]
    angle = freq * np.arange(rows)[None, :] * (np.pi / rows)
    cos, sin = np.cos(angle), np.sin(angle)
    sign = np.where(np.arange(rows) % 2 == 0, 1.0, -1.0)[:, None]
    own = np.concatenate([cos, sin], 0)
    behind = np.concatenate([sign * sin, -sign * cos], 0)
    back = own.T / rows
    return [jnp.asarray(t, F32).astype(BF16) for t in (own, behind, back)]


def dot(left, right):
    return jnp.dot(left, right, preferred_element_type=F32)


def split(value):
    high = value.astype(BF16)
    return high, (value - high.astype(F32)).astype(BF16)


def one_minus_exp(a):
    series = 1.0 - a / 9.0
    for k in (8.0, 7.0, 6.0, 5.0, 4.0, 3.0, 2.0):
        series = 1.0 - series * a / k
    return jnp.where(a < 0.5, a * series, 1.0 - jnp.exp(-a))


def column(row):
    rows = row.shape[1]
    eye = lax.broadcasted_iota(jnp.int32, (rows, rows), 0) == lax.broadcasted_iota(
        jnp.int32, (rows, rows), 1
    )
    return jnp.sum(jnp.where(eye, row, 0.0), axis=1, keepdims=True)


def scaled(tokens, scale, gain):
    return (tokens.astype(F32) * scale * gain).astype(BF16)


def spectral_product(data, filt):
    half = data.shape[0] // 2
    dc, ds, fc, fs = data[:half], data[half:], filt[:half], filt[half:]
    return jnp.concatenate([dc * fc - ds * fs, dc * fs + ds * fc], 0).astype(BF16)


def modes_over_rows(first, step, out_ref):
    rows, width = out_ref.shape
    for lane in range(0, width, LANES):
        cols = slice(lane, lane + LANES)
        term, ratio = first[:, :, cols], step[:, :, cols]
        for a in range(rows // SUB):
            out_ref[a * SUB : (a + 1) * SUB, cols] = jnp.sum(term, axis=0)
            if a + 1 < rows // SUB:
                term = term * ratio


def sublane_sums(parts):
    row = lax.broadcasted_iota(jnp.int32, parts[0].shape, 0)
    high = row >= 4
    parts = [
        jnp.where(high, b, a) + pltpu.roll(jnp.where(high, a, b), 4, 0)
        for a, b in zip(parts[:4], parts[4:])
    ]
    for shift in (2, 1):
        odd = lax.rem(row // shift, 2) == 1
        count = len(parts) // 2
        parts = [
            jnp.where(odd, b + pltpu.roll(b, shift, 0), a + pltpu.roll(a, SUB - shift, 0))
            for a, b in zip(parts[:count], parts[count:])
        ]
    return parts[0]


def end_totals(totals, signal, step):
    rows, width = signal.shape
    modes = step.shape[0]
    sums = {}
    for lane in range(0, width, LANES):
        cols = slice(lane, lane + LANES)
        tiles = [signal[r : r + SUB, cols] for r in range(0, rows, SUB)]
        for m in range(modes):
            total, rest = (tiles[0], tiles[1:]) if totals is None else (totals[lane, m], tiles)
            for tile in rest:
                total = total * step[m, :, cols] + tile
            sums[lane, m] = total
    return sums


def end_state(totals, last):
    modes, _, width = last.shape
    columns = []
    for lane in range(0, width, LANES):
        parts = [totals[lane, m] * last[m, :, lane : lane + LANES] for m in range(modes)]
        columns.append(
            jnp.concatenate([sublane_sums(parts[m : m + SUB]) for m in range(0, modes, SUB)], 0)
        )
    return jnp.concatenate(columns, 1)


def size(ref):
    return int(np.prod(ref.shape)) * ref.dtype.itemsize


def settle(span_ref, sem, total):
    part = span_ref.at[pl.ds(0, total // (LANES * 4))]
    pltpu.make_async_copy(part, part, sem).wait()


def hand_out(a_ref, b_ref, pa_ref, pb_ref, span_ref, sem):
    copies = [
        pltpu.make_async_copy(a_ref, pa_ref, sem),
        pltpu.make_async_copy(b_ref, pb_ref, sem),
    ]
    for copy in copies:
        copy.start()
    settle(span_ref, sem, size(a_ref) + size(b_ref))


def kernel(n, *refs):
    hbm = refs[:15]
    pa_ref, pb_ref = refs[15:17]
    vm = refs[17:32]
    (tail_ref, rim_ref, filt_ref, signal_ref, gated_ref) = refs[32:37]
    (own_ref, mate_ref, pair_ref, front_ref, rear_ref, extra_ref, span_ref) = refs[37:44]
    (queries_ref, short_ref, base_ref, through_ref, local_ref) = refs[44:49]
    (load_sem, rim_recv, mate_recv, far_recv, far_sem) = refs[49:]
    send_sem = load_sem.at[2]
    rows, width = vm[0].shape
    modes = vm[9].shape[0]

    groups = ((1, 2, 0), (3,), (12, 4, 13, 14), (15, 9, 10, 5, 6, 7, 8, 11))
    pairs_of = dict(enumerate(zip(hbm, vm)))
    keys = (slice(None), pl.ds(width, 2 * width))
    queries_only = (slice(None), pl.ds(0, width))
    pairs_of[3] = (hbm[3].at[keys], vm[3].at[keys])
    pairs_of[15] = (hbm[3].at[queries_only], vm[3].at[queries_only])
    loads = [
        [pltpu.make_async_copy(*pairs_of[i], load_sem.at[g]) for i in group]
        for g, group in enumerate(groups)
    ]

    def start(*which):
        for g in which:
            for load in loads[g]:
                load.start()

    def arrive(g):
        settle(span_ref, load_sem.at[g], sum(size(pairs_of[i][1]) for i in groups[g]))

    start(0, 1)
    me = lax.axis_index("seq")

    levels = n // QUAD
    level, place = me // QUAD, lax.rem(me, QUAD)
    base = level * QUAD
    mate = me + 1 - 2 * lax.rem(me, 2)
    speaker = (level == 0).astype(jnp.int32)
    front = place == speaker
    rear = place == 2
    speaks = jnp.logical_or(front, rear)
    barrier = pltpu.get_barrier_semaphore()

    def signal(sem, target):
        pl.semaphore_signal(sem, inc=1, device_id={"seq": target}, device_id_type=MESH)

    @pl.when(jnp.logical_and(place == 0, level > 0))
    def _():
        signal(barrier, me - 1)

    @pl.loop(1, QUAD)
    def _(i):
        signal(barrier, base + lax.rem(place + QUAD - i, QUAD))

    @pl.when(speaks)
    def _():
        @pl.loop(level + 1, levels)
        def _(i):
            signal(barrier, i * QUAD + 2)

    start(2, 3)
    (tok, rms_a, gain_a, proj_a, taps, out_a) = vm[:6]
    (rms_b, gain_b, proj_b, rates_ref, resid_ref, out_b, own_f, rim_f, back_f) = vm[6:]

    piece = rows // PIECES
    pieces = [pl.ds(p * piece, piece) for p in range(PIECES)]

    @pl.when(me == 0)
    def _():
        gated_ref[...] = jnp.zeros_like(gated_ref)
        for i, p in enumerate(pieces):
            pltpu.make_async_copy(gated_ref.at[p], rim_ref.at[p], rim_recv.at[i]).start()

    crossing = jnp.logical_and(place == QUAD - 1, level < levels - 1)

    @pl.when(rear)
    def _():
        pl.semaphore_wait(barrier, QUAD - 1 + 2 * level)

        @pl.loop(0, level)
        def _(i):
            credit = far_sem.at[(level == levels - 1).astype(jnp.int32)]
            signal(credit, i * QUAD + 2)
            signal(credit, i * QUAD + (i == 0).astype(jnp.int32))

    arrive(0)
    normed = scaled(tok[...], column(rms_a[...]), gain_a[...])
    arrive(1)
    pair_a = dot(normed, proj_a[:, width:])
    product = (pair_a[:, :width] * pair_a[:, width:]).astype(BF16)
    arrive(2)
    taps_spec = dot(own_f[...], taps[...])
    tail_ref[...] = dot(
        back_f[...], spectral_product(dot(rim_f[...], product), taps_spec)
    ).astype(BF16)

    @pl.when(jnp.logical_not(rear))
    def _():
        pl.semaphore_wait(barrier, QUAD - 1 + crossing.astype(jnp.int32))

    rim_copies = [
        pltpu.make_async_remote_copy(
            src_ref=tail_ref.at[p],
            dst_ref=rim_ref.at[p],
            send_sem=send_sem,
            recv_sem=rim_recv.at[i],
            device_id={"seq": lax.rem(me + 1, n)},
            device_id_type=MESH,
        )
        for i, p in enumerate(pieces)
    ]

    @pl.when(me < n - 1)
    def _():
        for copy in rim_copies:
            copy.start()

    arrive(3)
    queries_ref[...] = dot(normed, proj_a[:, :width])
    short_ref[...] = dot(back_f[...], spectral_product(dot(own_f[...], product), taps_spec))

    rates = rates_ref[...]
    length = float(n * rows)
    rates3 = jnp.broadcast_to(rates[:, None, :], (modes, SUB, width))
    within = lax.broadcasted_iota(jnp.int32, (modes, SUB, width), 1).astype(F32)
    step = jnp.exp(-rates3 * float(SUB))
    last = jnp.exp(-rates3 * (SUB - 1.0 - within))
    block = jnp.exp(-rates * float(rows))
    scale_b = column(rms_b[...])
    base_ref[...] = dot(scaled(tok[...], scale_b, gain_b[...]), proj_b[...])
    high, low = split(out_a[...].astype(F32) * gain_b[...])
    through_ref[...] = (dot(high, proj_b[...]) + dot(low, proj_b[...])).astype(BF16)

    totals = None
    for i, p in enumerate(pieces):
        rim_copies[i].wait_recv()
        span = slice(i * piece, (i + 1) * piece)
        gated = (queries_ref[p] * (short_ref[p] + rim_ref[p].astype(F32))).astype(BF16)
        gated_ref[p] = gated
        pair_b = base_ref[p, width:] + scale_b[span] * dot(gated, through_ref[:, width:])
        signal = (pair_b[:, :width] * pair_b[:, width:]).astype(BF16)
        signal_ref[p] = signal
        totals = end_totals(totals, signal.astype(F32), step)
    state = end_state(totals, last)
    own_ref[...] = state

    mate_copy = pltpu.make_async_remote_copy(
        src_ref=own_ref,
        dst_ref=mate_ref,
        send_sem=send_sem,
        recv_sem=mate_recv,
        device_id={"seq": mate},
        device_id_type=MESH,
    )
    mate_copy.start()

    def far_copy(slots, target, there):
        return pltpu.make_async_remote_copy(
            src_ref=pair_ref,
            dst_ref=slots.at[level],
            send_sem=send_sem,
            recv_sem=far_recv.at[(there - level <= 1).astype(jnp.int32)],
            device_id={"seq": target},
            device_id_type=MESH,
        )

    mate_copy.wait_recv()
    early = lax.rem(place, 2) == 0
    pair_ref[...] = (
        jnp.where(early, state, mate_ref[...]) * block + jnp.where(early, mate_ref[...], state)
    ).astype(BF16)

    @pl.when(front)
    def _():
        for i in (1, 0):
            far_copy(front_ref, base + 2 + i, level).start()

    def spread(slots, plan):
        for seat_there, last_level in plan:
            if seat_there is None:

                @pl.when(level < levels - (1 if last_level else 2))
                def _():
                    if last_level:
                        pl.semaphore_wait(far_sem.at[1], 1)
                    else:
                        pl.semaphore_wait(far_sem.at[0], levels - 2 - level)

            elif last_level:

                @pl.when(level < levels - 1)
                def _():
                    far_copy(slots, (levels - 1) * QUAD + seat_there, levels - 1).start()

            else:

                @pl.loop(level + 1, levels - 1)
                def _(there):
                    far_copy(slots, there * QUAD + seat_there, there).start()

    @pl.when(front)
    def _():
        spread(front_ref, FRONT_PLAN)

    @pl.when(rear)
    def _():
        spread(rear_ref, REAR_PLAN)

    pa_ref[...] = dot(gated_ref[...], out_a[...]).astype(BF16)
    queries_ref[...] = base_ref[:, :width] + scale_b * dot(gated_ref[...], through_ref[:, :width])
    length = float(n * rows)
    weights = resid_ref[...] * jnp.sqrt(
        one_minus_exp(2.0 * rates) / one_minus_exp(2.0 * rates * length)
    )
    modes_over_rows(weights[:, None, :] * jnp.exp(-rates3 * within), step, filt_ref)
    high, low = split(filt_ref[...])
    long_spec = dot(own_f[...], high) + dot(own_f[...], low)
    read = jnp.exp(-rates3 * (within + 1.0))
    two_blocks = jnp.exp(-rates * float(2 * rows))
    four_blocks = jnp.exp(-rates * float(4 * rows))
    seated = jnp.exp(-rates * (place * rows).astype(F32))
    local_ref[...] = dot(back_f[...], spectral_product(dot(own_f[...], signal_ref[...]), long_spec))

    extra_ref[...] = jnp.where(place == 0, jnp.zeros_like(state), mate_ref[...])

    always = size(rim_ref) + size(own_ref)
    letter = size(pair_ref)

    @pl.when(jnp.logical_and(jnp.logical_not(speaks), me < n - 1))
    def _():
        settle(span_ref, send_sem, always)

    @pl.when(me == n - 1)
    def _():
        settle(span_ref, send_sem, size(own_ref))

    for there in range(levels):
        rest = (levels - 1 - there) * QUAD

        @pl.when(jnp.logical_and(front, level == there))
        def _():
            settle(span_ref, send_sem, always + (rest + 2) * letter)

        @pl.when(jnp.logical_and(rear, level == there))
        def _():
            settle(span_ref, send_sem, always + rest * letter)

    def gather(source, total):
        pairs = front_ref[source].astype(F32) * two_blocks
        return total * four_blocks + (pairs + rear_ref[source].astype(F32))

    older = jnp.maximum(level - 1, 0)
    for there in range(2, levels):

        @pl.when(level == there)
        def _():
            settle(span_ref, far_recv.at[0], 2 * (there - 1) * letter)

    total = lax.fori_loop(0, older, gather, jnp.zeros((modes, width), F32))
    back = place >= 2

    @pl.when(jnp.logical_and(level > 0, jnp.logical_not(back)))
    def _():
        settle(span_ref, far_recv.at[1], 2 * letter)

    @pl.when(jnp.logical_and(level > 0, back))
    def _():
        settle(span_ref, far_recv.at[1], 3 * letter)

    @pl.when(jnp.logical_and(level == 0, back))
    def _():
        settle(span_ref, far_recv.at[1], letter)

    total = lax.fori_loop(older, level, gather, total)

    @pl.when(place >= 2)
    def _():
        pairs = front_ref[level].astype(F32)
        extra_ref[...] = jnp.where(place == 2, pairs, pairs * block + extra_ref[...])

    total = total * seated + extra_ref[...]
    modes_over_rows((total * weights)[:, None, :] * read, step, filt_ref)
    long_out = (local_ref[...] + filt_ref[...]).astype(BF16)
    gated_b = (queries_ref[...] * long_out.astype(F32)).astype(BF16)
    pb_ref[...] = dot(gated_b, out_b[...]).astype(BF16)


def solution(mesh):
    n = mesh.shape["seq"]
    assert n % QUAD == 0

    def on_device(*args):
        rows, width = args[0].shape
        modes = args[9].shape[0]
        args = [a[None] if a.ndim == 1 else a for a in args] + dft_tables(rows)
        block = jax.ShapeDtypeStruct((rows, width), BF16)
        span = sum(size(a) for a in args) + (n + 8) * modes * width * 2
        fast = pltpu.VMEM((rows, width), BF16)
        inside = pl.BlockSpec(memory_space=pltpu.VMEM)
        anywhere = pl.BlockSpec(memory_space=pl.ANY)
        results = pl.pallas_call(
            functools.partial(kernel, n),
            out_shape=(fast, fast),
            in_specs=[anywhere] * len(args),
            out_specs=(inside, inside),
            scratch_shapes=[pltpu.VMEM(a.shape, a.dtype) for a in args]
            + [
                pltpu.VMEM((rows, width), BF16),
                pltpu.VMEM((rows, width), BF16),
                pltpu.VMEM((rows, width), F32),
                pltpu.VMEM((rows, width), BF16),
                pltpu.VMEM((rows, width), BF16),
                pltpu.VMEM((modes, width), F32),
                pltpu.VMEM((modes, width), F32),
                pltpu.VMEM((modes, width), BF16),
                pltpu.VMEM((n // QUAD, modes, width), BF16),
                pltpu.VMEM((n // QUAD, modes, width), BF16),
                pltpu.VMEM((modes, width), F32),
                pltpu.VMEM((span // (4 * LANES), 1, LANES), F32),
                pltpu.VMEM((rows, width), F32),
                pltpu.VMEM((rows, width), F32),
                pltpu.VMEM((rows, 3 * width), F32),
                pltpu.VMEM((width, 3 * width), BF16),
                pltpu.VMEM((rows, width), F32),
                pltpu.SemaphoreType.DMA((4,)),
                pltpu.SemaphoreType.DMA((PIECES,)),
                pltpu.SemaphoreType.DMA,
                pltpu.SemaphoreType.DMA((2,)),
                pltpu.SemaphoreType.REGULAR((2,)),
            ],
            compiler_params=pltpu.CompilerParams(collective_id=0, has_side_effects=True),
        )(*args)
        return pl.pallas_call(
            hand_out,
            out_shape=(block, block),
            in_specs=[inside] * 2,
            out_specs=(anywhere, anywhere),
            scratch_shapes=[
                pltpu.VMEM((2 * rows * width * 2 // (4 * LANES), 1, LANES), F32),
                pltpu.SemaphoreType.DMA,
            ],
        )(*[pltpu.with_memory_space_constraint(r, pltpu.VMEM) for r in results])

    shard = P(("groups", "seq"))
    wide = P(("groups", "seq"), None)
    placed = (wide, shard, P(), P(), P(), P(), shard, P(), P(), P(), P(), P())
    return jax.shard_map(
        on_device, mesh=mesh, in_specs=placed, out_specs=(wide, wide), check_vma=False
    )
```

```python
import functools

import jax
import jax.numpy as jnp
import numpy as np
from jax import lax
from jax.experimental import pallas as pl
from jax.experimental.pallas import tpu as pltpu
from jax.sharding import PartitionSpec as P

MESH = pl.DeviceIdType.MESH
F32 = jnp.float32
BF16 = jnp.bfloat16
SUB = 8
LANES = 128
QUAD = 4
PIECES = 2
FRONT_PLAN = [(None, 0), (3, 0), (1, 0), (2, 0), (0, 0), (None, 1), (3, 1), (1, 1), (2, 1), (0, 1)]
REAR_PLAN = [(None, 0), (None, 1), (1, 1), (1, 0), (0, 0), (0, 1), (3, 1), (3, 0), (2, 1), (2, 0)]


def dft_tables(rows):
    freq = (np.arange(rows) + 0.5)[:, None]
    angle = freq * np.arange(rows)[None, :] * (np.pi / rows)
    cos, sin = np.cos(angle), np.sin(angle)
    sign = np.where(np.arange(rows) % 2 == 0, 1.0, -1.0)[:, None]
    own = np.concatenate([cos, sin], 0)
    behind = np.concatenate([sign * sin, -sign * cos], 0)
    back = own.T / rows
    return [jnp.asarray(t, F32).astype(BF16) for t in (own, behind, back)]


def dot(left, right):
    return jnp.dot(left, right, preferred_element_type=F32)


def split(value):
    high = value.astype(BF16)
    return high, (value - high.astype(F32)).astype(BF16)


def one_minus_exp(a):
    series = 1.0 - a / 9.0
    for k in (8.0, 7.0, 6.0, 5.0, 4.0, 3.0, 2.0):
        series = 1.0 - series * a / k
    return jnp.where(a < 0.5, a * series, 1.0 - jnp.exp(-a))


def column(row):
    rows = row.shape[1]
    eye = lax.broadcasted_iota(jnp.int32, (rows, rows), 0) == lax.broadcasted_iota(
        jnp.int32, (rows, rows), 1
    )
    return jnp.sum(jnp.where(eye, row, 0.0), axis=1, keepdims=True)


def scaled(tokens, scale, gain):
    return (tokens.astype(F32) * scale * gain).astype(BF16)


def spectral_product(data, filt):
    half = data.shape[0] // 2
    dc, ds, fc, fs = data[:half], data[half:], filt[:half], filt[half:]
    return jnp.concatenate([dc * fc - ds * fs, dc * fs + ds * fc], 0).astype(BF16)


def modes_over_rows(first, step, out_ref):
    rows, width = out_ref.shape
    for lane in range(0, width, LANES):
        cols = slice(lane, lane + LANES)
        term, ratio = first[:, :, cols], step[:, :, cols]
        for a in range(rows // SUB):
            out_ref[a * SUB : (a + 1) * SUB, cols] = jnp.sum(term, axis=0)
            if a + 1 < rows // SUB:
                term = term * ratio


def sublane_sums(parts):
    row = lax.broadcasted_iota(jnp.int32, parts[0].shape, 0)
    high = row >= 4
    parts = [
        jnp.where(high, b, a) + pltpu.roll(jnp.where(high, a, b), 4, 0)
        for a, b in zip(parts[:4], parts[4:])
    ]
    for shift in (2, 1):
        odd = lax.rem(row // shift, 2) == 1
        count = len(parts) // 2
        parts = [
            jnp.where(odd, b + pltpu.roll(b, shift, 0), a + pltpu.roll(a, SUB - shift, 0))
            for a, b in zip(parts[:count], parts[count:])
        ]
    return parts[0]


def end_totals(totals, signal, step):
    rows, width = signal.shape
    modes = step.shape[0]
    sums = {}
    for lane in range(0, width, LANES):
        cols = slice(lane, lane + LANES)
        tiles = [signal[r : r + SUB, cols] for r in range(0, rows, SUB)]
        for m in range(modes):
            total, rest = (tiles[0], tiles[1:]) if totals is None else (totals[lane, m], tiles)
            for tile in rest:
                total = total * step[m, :, cols] + tile
            sums[lane, m] = total
    return sums


def end_state(totals, last):
    modes, _, width = last.shape
    columns = []
    for lane in range(0, width, LANES):
        parts = [totals[lane, m] * last[m, :, lane : lane + LANES] for m in range(modes)]
        columns.append(
            jnp.concatenate([sublane_sums(parts[m : m + SUB]) for m in range(0, modes, SUB)], 0)
        )
    return jnp.concatenate(columns, 1)


def size(ref):
    return int(np.prod(ref.shape)) * ref.dtype.itemsize


def settle(span_ref, sem, total):
    part = span_ref.at[pl.ds(0, total // (LANES * 4))]
    pltpu.make_async_copy(part, part, sem).wait()


def hand_out(a_ref, b_ref, pa_ref, pb_ref, span_ref, sem):
    copies = [
        pltpu.make_async_copy(a_ref, pa_ref, sem),
        pltpu.make_async_copy(b_ref, pb_ref, sem),
    ]
    for copy in copies:
        copy.start()
    settle(span_ref, sem, size(a_ref) + size(b_ref))


def kernel(n, *refs):
    hbm = refs[:15]
    pa_ref, pb_ref = refs[15:17]
    vm = refs[17:32]
    (tail_ref, rim_ref, filt_ref, signal_ref, gated_ref) = refs[32:37]
    (own_ref, mate_ref, pair_ref, front_ref, rear_ref, span_ref) = refs[37:43]
    (queries_ref, short_ref, base_ref, through_ref, local_ref) = refs[43:48]
    (load_sem, rim_recv, mate_recv, far_recv, far_sem) = refs[48:]
    send_sem = load_sem.at[2]
    rows, width = vm[0].shape
    modes = vm[9].shape[0]

    groups = ((1, 2, 0), (3,), (12, 4, 13, 14), (15, 9, 10, 5, 6, 7, 8, 11))
    pairs_of = dict(enumerate(zip(hbm, vm)))
    keys = (slice(None), pl.ds(width, 2 * width))
    queries_only = (slice(None), pl.ds(0, width))
    pairs_of[3] = (hbm[3].at[keys], vm[3].at[keys])
    pairs_of[15] = (hbm[3].at[queries_only], vm[3].at[queries_only])
    loads = [
        [pltpu.make_async_copy(*pairs_of[i], load_sem.at[g]) for i in group]
        for g, group in enumerate(groups)
    ]

    def start(*which):
        for g in which:
            for load in loads[g]:
                load.start()

    def arrive(g):
        settle(span_ref, load_sem.at[g], sum(size(pairs_of[i][1]) for i in groups[g]))

    start(0, 1)
    me = lax.axis_index("seq")

    levels = n // QUAD
    level, place = me // QUAD, lax.rem(me, QUAD)
    base = level * QUAD
    mate = me + 1 - 2 * lax.rem(me, 2)
    speaker = (level == 0).astype(jnp.int32)
    front = place == speaker
    rear = place == 2
    speaks = jnp.logical_or(front, rear)
    barrier = pltpu.get_barrier_semaphore()

    def signal(sem, target):
        pl.semaphore_signal(sem, inc=1, device_id={"seq": target}, device_id_type=MESH)

    @pl.when(jnp.logical_and(place == 0, level > 0))
    def _():
        signal(barrier, me - 1)

    @pl.loop(1, QUAD)
    def _(i):
        signal(barrier, base + lax.rem(place + QUAD - i, QUAD))

    @pl.when(speaks)
    def _():
        @pl.loop(level + 1, levels)
        def _(i):
            signal(barrier, i * QUAD + 2)

    start(2, 3)
    (tok, rms_a, gain_a, proj_a, taps, out_a) = vm[:6]
    (rms_b, gain_b, proj_b, rates_ref, resid_ref, out_b, own_f, rim_f, back_f) = vm[6:]

    piece = rows // PIECES
    pieces = [pl.ds(p * piece, piece) for p in range(PIECES)]

    @pl.when(me == 0)
    def _():
        gated_ref[...] = jnp.zeros_like(gated_ref)
        for i, p in enumerate(pieces):
            pltpu.make_async_copy(gated_ref.at[p], rim_ref.at[p], rim_recv.at[i]).start()

    crossing = jnp.logical_and(place == QUAD - 1, level < levels - 1)

    @pl.when(rear)
    def _():
        pl.semaphore_wait(barrier, QUAD - 1 + 2 * level)

        @pl.loop(0, level)
        def _(i):
            credit = far_sem.at[(level == levels - 1).astype(jnp.int32)]
            signal(credit, i * QUAD + 2)
            signal(credit, i * QUAD + (i == 0).astype(jnp.int32))

    arrive(0)
    normed = scaled(tok[...], column(rms_a[...]), gain_a[...])
    arrive(1)
    pair_a = dot(normed, proj_a[:, width:])
    product = (pair_a[:, :width] * pair_a[:, width:]).astype(BF16)
    arrive(2)
    taps_spec = dot(own_f[...], taps[...])
    tail_ref[...] = dot(
        back_f[...], spectral_product(dot(rim_f[...], product), taps_spec)
    ).astype(BF16)

    @pl.when(jnp.logical_not(rear))
    def _():
        pl.semaphore_wait(barrier, QUAD - 1 + crossing.astype(jnp.int32))

    rim_copies = [
        pltpu.make_async_remote_copy(
            src_ref=tail_ref.at[p],
            dst_ref=rim_ref.at[p],
            send_sem=send_sem,
            recv_sem=rim_recv.at[i],
            device_id={"seq": lax.rem(me + 1, n)},
            device_id_type=MESH,
        )
        for i, p in enumerate(pieces)
    ]

    @pl.when(me < n - 1)
    def _():
        for copy in rim_copies:
            copy.start()

    arrive(3)
    queries_ref[...] = dot(normed, proj_a[:, :width])
    short_ref[...] = dot(back_f[...], spectral_product(dot(own_f[...], product), taps_spec))

    rates = rates_ref[...]
    length = float(n * rows)
    rates3 = jnp.broadcast_to(rates[:, None, :], (modes, SUB, width))
    within = lax.broadcasted_iota(jnp.int32, (modes, SUB, width), 1).astype(F32)
    step = jnp.exp(-rates3 * float(SUB))
    last = jnp.exp(-rates3 * (SUB - 1.0 - within))
    block = jnp.exp(-rates * float(rows))
    scale_b = column(rms_b[...])
    base_ref[...] = dot(scaled(tok[...], scale_b, gain_b[...]), proj_b[...])
    high, low = split(out_a[...].astype(F32) * gain_b[...])
    through_ref[...] = (dot(high, proj_b[...]) + dot(low, proj_b[...])).astype(BF16)

    totals = None
    for i, p in enumerate(pieces):
        rim_copies[i].wait_recv()
        span = slice(i * piece, (i + 1) * piece)
        gated = (queries_ref[p] * (short_ref[p] + rim_ref[p].astype(F32))).astype(BF16)
        gated_ref[p] = gated
        pair_b = base_ref[p, width:] + scale_b[span] * dot(gated, through_ref[:, width:])
        signal = (pair_b[:, :width] * pair_b[:, width:]).astype(BF16)
        signal_ref[p] = signal
        totals = end_totals(totals, signal.astype(F32), step)
    state = end_state(totals, last)
    own_ref[...] = state

    mate_copy = pltpu.make_async_remote_copy(
        src_ref=own_ref,
        dst_ref=mate_ref,
        send_sem=send_sem,
        recv_sem=mate_recv,
        device_id={"seq": mate},
        device_id_type=MESH,
    )
    mate_copy.start()

    def far_copy(slots, target, there):
        return pltpu.make_async_remote_copy(
            src_ref=pair_ref,
            dst_ref=slots.at[level],
            send_sem=send_sem,
            recv_sem=far_recv.at[(there - level <= 1).astype(jnp.int32)],
            device_id={"seq": target},
            device_id_type=MESH,
        )

    mate_copy.wait_recv()
    early = lax.rem(place, 2) == 0
    pair_ref[...] = (
        jnp.where(early, state, mate_ref[...]) * block + jnp.where(early, mate_ref[...], state)
    ).astype(BF16)

    def spread(slots, plan):
        for seat_there, last_level in plan:
            if seat_there is None:

                @pl.when(level < levels - (1 if last_level else 2))
                def _():
                    if last_level:
                        pl.semaphore_wait(far_sem.at[1], 1)
                    else:
                        pl.semaphore_wait(far_sem.at[0], levels - 2 - level)

            elif last_level:

                @pl.when(level < levels - 1)
                def _():
                    far_copy(slots, (levels - 1) * QUAD + seat_there, levels - 1).start()

            else:

                @pl.loop(level + 1, levels - 1)
                def _(there):
                    far_copy(slots, there * QUAD + seat_there, there).start()

    @pl.when(front)
    def _():
        spread(front_ref, FRONT_PLAN)
        for i in (1, 0):
            far_copy(front_ref, base + 2 + i, level).start()

    @pl.when(rear)
    def _():
        spread(rear_ref, REAR_PLAN)

    pa_ref[...] = dot(gated_ref[...], out_a[...]).astype(BF16)
    queries_ref[...] = base_ref[:, :width] + scale_b * dot(gated_ref[...], through_ref[:, :width])
    length = float(n * rows)
    weights = resid_ref[...] * jnp.sqrt(
        one_minus_exp(2.0 * rates) / one_minus_exp(2.0 * rates * length)
    )
    modes_over_rows(weights[:, None, :] * jnp.exp(-rates3 * within), step, filt_ref)
    high, low = split(filt_ref[...])
    long_spec = dot(own_f[...], high) + dot(own_f[...], low)
    read = jnp.exp(-rates3 * (within + 1.0))
    two_blocks = jnp.exp(-rates * float(2 * rows))
    four_blocks = jnp.exp(-rates * float(4 * rows))
    seated = jnp.exp(-rates * (place * rows).astype(F32))
    local_ref[...] = dot(back_f[...], spectral_product(dot(own_f[...], signal_ref[...]), long_spec))

    always = size(rim_ref) + size(own_ref)
    letter = size(pair_ref)

    @pl.when(jnp.logical_and(jnp.logical_not(speaks), me < n - 1))
    def _():
        settle(span_ref, send_sem, always)

    @pl.when(me == n - 1)
    def _():
        settle(span_ref, send_sem, size(own_ref))

    for there in range(levels):
        rest = (levels - 1 - there) * QUAD

        @pl.when(jnp.logical_and(front, level == there))
        def _():
            settle(span_ref, send_sem, always + (rest + 2) * letter)

        @pl.when(jnp.logical_and(rear, level == there))
        def _():
            settle(span_ref, send_sem, always + rest * letter)

    def gather(source, total):
        pairs = front_ref[source].astype(F32) * two_blocks
        return total * four_blocks + (pairs + rear_ref[source].astype(F32))

    older = jnp.maximum(level - 1, 0)
    for there in range(2, levels):

        @pl.when(level == there)
        def _():
            settle(span_ref, far_recv.at[0], 2 * (there - 1) * letter)

    total = lax.fori_loop(0, older, gather, jnp.zeros((modes, width), F32))
    back = place >= 2

    @pl.when(jnp.logical_and(level > 0, jnp.logical_not(back)))
    def _():
        settle(span_ref, far_recv.at[1], 2 * letter)

    @pl.when(jnp.logical_and(level > 0, back))
    def _():
        settle(span_ref, far_recv.at[1], 3 * letter)

    @pl.when(jnp.logical_and(level == 0, back))
    def _():
        settle(span_ref, far_recv.at[1], letter)

    total = jnp.where(level > 0, gather(older, total), 0.0) * seated
    pairs = front_ref[level].astype(F32)
    extra = jnp.where(place == 0, 0.0, mate_ref[...])
    extra = jnp.where(place < 2, extra, jnp.where(place == 2, pairs, pairs * block + extra))
    total = total + extra
    modes_over_rows((total * weights)[:, None, :] * read, step, filt_ref)
    long_out = (local_ref[...] + filt_ref[...]).astype(BF16)
    gated_b = (queries_ref[...] * long_out.astype(F32)).astype(BF16)
    pb_ref[...] = dot(gated_b, out_b[...]).astype(BF16)


def solution(mesh):
    n = mesh.shape["seq"]
    assert n % QUAD == 0

    def on_device(*args):
        rows, width = args[0].shape
        modes = args[9].shape[0]
        args = [a[None] if a.ndim == 1 else a for a in args] + dft_tables(rows)
        block = jax.ShapeDtypeStruct((rows, width), BF16)
        span = sum(size(a) for a in args) + (n + 8) * modes * width * 2
        fast = pltpu.VMEM((rows, width), BF16)
        inside = pl.BlockSpec(memory_space=pltpu.VMEM)
        anywhere = pl.BlockSpec(memory_space=pl.ANY)
        results = pl.pallas_call(
            functools.partial(kernel, n),
            out_shape=(fast, fast),
            in_specs=[anywhere] * len(args),
            out_specs=(inside, inside),
            scratch_shapes=[pltpu.VMEM(a.shape, a.dtype) for a in args]
            + [
                pltpu.VMEM((rows, width), BF16),
                pltpu.VMEM((rows, width), BF16),
                pltpu.VMEM((rows, width), F32),
                pltpu.VMEM((rows, width), BF16),
                pltpu.VMEM((rows, width), BF16),
                pltpu.VMEM((modes, width), F32),
                pltpu.VMEM((modes, width), F32),
                pltpu.VMEM((modes, width), BF16),
                pltpu.VMEM((n // QUAD, modes, width), BF16),
                pltpu.VMEM((n // QUAD, modes, width), BF16),
                pltpu.VMEM((span // (4 * LANES), 1, LANES), F32),
                pltpu.VMEM((rows, width), F32),
                pltpu.VMEM((rows, width), F32),
                pltpu.VMEM((rows, 3 * width), F32),
                pltpu.VMEM((width, 3 * width), BF16),
                pltpu.VMEM((rows, width), F32),
                pltpu.SemaphoreType.DMA((4,)),
                pltpu.SemaphoreType.DMA((PIECES,)),
                pltpu.SemaphoreType.DMA,
                pltpu.SemaphoreType.DMA((2,)),
                pltpu.SemaphoreType.REGULAR((2,)),
            ],
            compiler_params=pltpu.CompilerParams(collective_id=0, has_side_effects=True),
        )(*args)
        return pl.pallas_call(
            hand_out,
            out_shape=(block, block),
            in_specs=[inside] * 2,
            out_specs=(anywhere, anywhere),
            scratch_shapes=[
                pltpu.VMEM((2 * rows * width * 2 // (4 * LANES), 1, LANES), F32),
                pltpu.SemaphoreType.DMA,
            ],
        )(*[pltpu.with_memory_space_constraint(r, pltpu.VMEM) for r in results])

    shard = P(("groups", "seq"))
    wide = P(("groups", "seq"), None)
    placed = (wide, shard, P(), P(), P(), P(), shard, P(), P(), P(), P(), P())
    return jax.shard_map(
        on_device, mesh=mesh, in_specs=placed, out_specs=(wide, wide), check_vma=False
    )
```

```python
import functools

import jax
import jax.numpy as jnp
import numpy as np
from jax import lax
from jax.experimental import pallas as pl
from jax.experimental.pallas import tpu as pltpu
from jax.sharding import PartitionSpec as P

MESH = pl.DeviceIdType.MESH
F32 = jnp.float32
BF16 = jnp.bfloat16
SUB = 8
LANES = 128
QUAD = 4
PIECES = 2
FRONT_PLAN = [(None, 0), (3, 0), (1, 0), (2, 0), (0, 0), (None, 1), (3, 1), (1, 1), (2, 1), (0, 1)]
REAR_PLAN = [(None, 0), (None, 1), (1, 1), (1, 0), (0, 0), (0, 1), (3, 1), (3, 0), (2, 1), (2, 0)]


def dft_tables(rows):
    freq = (np.arange(rows) + 0.5)[:, None]
    angle = freq * np.arange(rows)[None, :] * (np.pi / rows)
    cos, sin = np.cos(angle), np.sin(angle)
    sign = np.where(np.arange(rows) % 2 == 0, 1.0, -1.0)[:, None]
    own = np.concatenate([cos, sin], 0)
    behind = np.concatenate([sign * sin, -sign * cos], 0)
    back = own.T / rows
    return [jnp.asarray(t, F32).astype(BF16) for t in (own, behind, back)]


def dot(left, right):
    return jnp.dot(left, right, preferred_element_type=F32)


def split(value):
    high = value.astype(BF16)
    return high, (value - high.astype(F32)).astype(BF16)


def one_minus_exp(a):
    series = 1.0 - a / 9.0
    for k in (8.0, 7.0, 6.0, 5.0, 4.0, 3.0, 2.0):
        series = 1.0 - series * a / k
    return jnp.where(a < 0.5, a * series, 1.0 - jnp.exp(-a))


def column(row):
    rows = row.shape[1]
    eye = lax.broadcasted_iota(jnp.int32, (rows, rows), 0) == lax.broadcasted_iota(
        jnp.int32, (rows, rows), 1
    )
    return jnp.sum(jnp.where(eye, row, 0.0), axis=1, keepdims=True)


def scaled(tokens, scale, gain):
    return (tokens.astype(F32) * scale * gain).astype(BF16)


def spectral_product(data, filt):
    half = data.shape[0] // 2
    dc, ds, fc, fs = data[:half], data[half:], filt[:half], filt[half:]
    return jnp.concatenate([dc * fc - ds * fs, dc * fs + ds * fc], 0).astype(BF16)


def modes_over_rows(first, step, out_ref):
    rows, width = out_ref.shape
    for lane in range(0, width, LANES):
        cols = slice(lane, lane + LANES)
        term, ratio = first[:, :, cols], step[:, :, cols]
        for a in range(rows // SUB):
            out_ref[a * SUB : (a + 1) * SUB, cols] = jnp.sum(term, axis=0)
            if a + 1 < rows // SUB:
                term = term * ratio


def sublane_sums(parts):
    row = lax.broadcasted_iota(jnp.int32, parts[0].shape, 0)
    high = row >= 4
    parts = [
        jnp.where(high, b, a) + pltpu.roll(jnp.where(high, a, b), 4, 0)
        for a, b in zip(parts[:4], parts[4:])
    ]
    for shift in (2, 1):
        odd = lax.rem(row // shift, 2) == 1
        count = len(parts) // 2
        parts = [
            jnp.where(odd, b + pltpu.roll(b, shift, 0), a + pltpu.roll(a, SUB - shift, 0))
            for a, b in zip(parts[:count], parts[count:])
        ]
    return parts[0]


def end_totals(totals, signal, step):
    rows, width = signal.shape
    modes = step.shape[0]
    sums = {}
    for lane in range(0, width, LANES):
        cols = slice(lane, lane + LANES)
        tiles = [signal[r : r + SUB, cols] for r in range(0, rows, SUB)]
        for m in range(modes):
            total, rest = (tiles[0], tiles[1:]) if totals is None else (totals[lane, m], tiles)
            for tile in rest:
                total = total * step[m, :, cols] + tile
            sums[lane, m] = total
    return sums


def end_state(totals, last):
    modes, _, width = last.shape
    columns = []
    for lane in range(0, width, LANES):
        parts = [totals[lane, m] * last[m, :, lane : lane + LANES] for m in range(modes)]
        columns.append(
            jnp.concatenate([sublane_sums(parts[m : m + SUB]) for m in range(0, modes, SUB)], 0)
        )
    return jnp.concatenate(columns, 1)


def size(ref):
    return int(np.prod(ref.shape)) * ref.dtype.itemsize


def settle(span_ref, sem, total):
    part = span_ref.at[pl.ds(0, total // (LANES * 4))]
    pltpu.make_async_copy(part, part, sem).wait()


def hand_out(a_ref, b_ref, pa_ref, pb_ref, span_ref, sem):
    copies = [
        pltpu.make_async_copy(a_ref, pa_ref, sem),
        pltpu.make_async_copy(b_ref, pb_ref, sem),
    ]
    for copy in copies:
        copy.start()
    settle(span_ref, sem, size(a_ref) + size(b_ref))


def kernel(n, *refs):
    hbm = refs[:15]
    pa_ref, pb_ref = refs[15:17]
    vm = refs[17:32]
    (tail_ref, rim_ref, filt_ref, signal_ref, gated_ref) = refs[32:37]
    (own_ref, mate_ref, pair_ref, front_ref, rear_ref, span_ref) = refs[37:43]
    (queries_ref, short_ref, base_ref, through_ref, local_ref) = refs[43:48]
    (load_sem, rim_recv, mate_recv, far_recv, far_sem) = refs[48:]
    send_sem = load_sem.at[2]
    rows, width = vm[0].shape
    modes = vm[9].shape[0]

    groups = ((1, 2, 0), (3,), (12, 4, 13, 14), (15, 9, 10, 5, 6, 7, 8, 11))
    pairs_of = dict(enumerate(zip(hbm, vm)))
    keys = (slice(None), pl.ds(width, 2 * width))
    queries_only = (slice(None), pl.ds(0, width))
    pairs_of[3] = (hbm[3].at[keys], vm[3].at[keys])
    pairs_of[15] = (hbm[3].at[queries_only], vm[3].at[queries_only])
    loads = [
        [pltpu.make_async_copy(*pairs_of[i], load_sem.at[g]) for i in group]
        for g, group in enumerate(groups)
    ]

    def start(*which):
        for g in which:
            for load in loads[g]:
                load.start()

    def arrive(g):
        settle(span_ref, load_sem.at[g], sum(size(pairs_of[i][1]) for i in groups[g]))

    start(0, 1)
    me = lax.axis_index("seq")

    levels = n // QUAD
    level, place = me // QUAD, lax.rem(me, QUAD)
    base = level * QUAD
    mate = me + 1 - 2 * lax.rem(me, 2)
    speaker = (level == 0).astype(jnp.int32)
    front = place == speaker
    rear = place == 2
    speaks = jnp.logical_or(front, rear)
    barrier = pltpu.get_barrier_semaphore()

    def signal(sem, target):
        pl.semaphore_signal(sem, inc=1, device_id={"seq": target}, device_id_type=MESH)

    @pl.when(jnp.logical_and(place == 0, level > 0))
    def _():
        signal(barrier, me - 1)

    @pl.loop(1, QUAD)
    def _(i):
        signal(barrier, base + lax.rem(place + QUAD - i, QUAD))

    @pl.when(speaks)
    def _():
        @pl.loop(level + 1, levels)
        def _(i):
            signal(barrier, i * QUAD + 2)

    start(2)
    (tok, rms_a, gain_a, proj_a, taps, out_a) = vm[:6]
    (rms_b, gain_b, proj_b, rates_ref, resid_ref, out_b, own_f, rim_f, back_f) = vm[6:]

    cut = rows * 5 // 8
    spans = ((0, cut), (cut, rows))
    pieces = [pl.ds(a, b - a) for a, b in spans]

    @pl.when(me == 0)
    def _():
        gated_ref[...] = jnp.zeros_like(gated_ref)
        for i, p in enumerate(pieces):
            pltpu.make_async_copy(gated_ref.at[p], rim_ref.at[p], rim_recv.at[i]).start()

    crossing = jnp.logical_and(place == QUAD - 1, level < levels - 1)

    @pl.when(rear)
    def _():
        pl.semaphore_wait(barrier, QUAD - 1 + 2 * level)

        @pl.loop(0, level)
        def _(i):
            credit = far_sem.at[(level == levels - 1).astype(jnp.int32)]
            signal(credit, i * QUAD + 2)
            signal(credit, i * QUAD + (i == 0).astype(jnp.int32))

    arrive(0)
    normed = scaled(tok[...], column(rms_a[...]), gain_a[...])
    arrive(1)
    start(3)
    pair_a = dot(normed, proj_a[:, width:])
    product = (pair_a[:, :width] * pair_a[:, width:]).astype(BF16)
    arrive(2)
    taps_spec = dot(own_f[...], taps[...])
    tail_ref[...] = dot(
        back_f[...], spectral_product(dot(rim_f[...], product), taps_spec)
    ).astype(BF16)

    @pl.when(jnp.logical_not(rear))
    def _():
        pl.semaphore_wait(barrier, QUAD - 1 + crossing.astype(jnp.int32))

    rim_copies = [
        pltpu.make_async_remote_copy(
            src_ref=tail_ref.at[p],
            dst_ref=rim_ref.at[p],
            send_sem=send_sem,
            recv_sem=rim_recv.at[i],
            device_id={"seq": lax.rem(me + 1, n)},
            device_id_type=MESH,
        )
        for i, p in enumerate(pieces)
    ]

    @pl.when(me < n - 1)
    def _():
        for copy in rim_copies:
            copy.start()

    arrive(3)
    queries_ref[...] = dot(normed, proj_a[:, :width])
    short_ref[...] = dot(back_f[...], spectral_product(dot(own_f[...], product), taps_spec))

    rates = rates_ref[...]
    length = float(n * rows)
    rates3 = jnp.broadcast_to(rates[:, None, :], (modes, SUB, width))
    within = lax.broadcasted_iota(jnp.int32, (modes, SUB, width), 1).astype(F32)
    step = jnp.exp(-rates3 * float(SUB))
    last = jnp.exp(-rates3 * (SUB - 1.0 - within))
    block = jnp.exp(-rates * float(rows))
    scale_b = column(rms_b[...])
    base_ref[...] = dot(scaled(tok[...], scale_b, gain_b[...]), proj_b[...])
    high, low = split(out_a[...].astype(F32) * gain_b[...])
    through_ref[...] = (dot(high, proj_b[...]) + dot(low, proj_b[...])).astype(BF16)

    totals = None
    for i, p in enumerate(pieces):
        rim_copies[i].wait_recv()
        span = slice(*spans[i])
        gated = (queries_ref[p] * (short_ref[p] + rim_ref[p].astype(F32))).astype(BF16)
        gated_ref[p] = gated
        pair_b = base_ref[p, width:] + scale_b[span] * dot(gated, through_ref[:, width:])
        signal = (pair_b[:, :width] * pair_b[:, width:]).astype(BF16)
        signal_ref[p] = signal
        totals = end_totals(totals, signal.astype(F32), step)
    state = end_state(totals, last)
    own_ref[...] = state

    mate_copy = pltpu.make_async_remote_copy(
        src_ref=own_ref,
        dst_ref=mate_ref,
        send_sem=send_sem,
        recv_sem=mate_recv,
        device_id={"seq": mate},
        device_id_type=MESH,
    )
    mate_copy.start()

    def far_copy(slots, target, there):
        return pltpu.make_async_remote_copy(
            src_ref=pair_ref,
            dst_ref=slots.at[level],
            send_sem=send_sem,
            recv_sem=far_recv.at[(there - level <= 1).astype(jnp.int32)],
            device_id={"seq": target},
            device_id_type=MESH,
        )

    mate_copy.wait_recv()
    early = lax.rem(place, 2) == 0
    pair_ref[...] = (
        jnp.where(early, state, mate_ref[...]) * block + jnp.where(early, mate_ref[...], state)
    ).astype(BF16)

    def spread(slots, plan):
        for seat_there, last_level in plan:
            if seat_there is None:

                @pl.when(level < levels - (1 if last_level else 2))
                def _():
                    if last_level:
                        pl.semaphore_wait(far_sem.at[1], 1)
                    else:
                        pl.semaphore_wait(far_sem.at[0], levels - 2 - level)

            elif last_level:

                @pl.when(level < levels - 1)
                def _():
                    far_copy(slots, (levels - 1) * QUAD + seat_there, levels - 1).start()

            else:

                @pl.loop(level + 1, levels - 1)
                def _(there):
                    far_copy(slots, there * QUAD + seat_there, there).start()

    @pl.when(front)
    def _():
        spread(front_ref, FRONT_PLAN)
        for i in (1, 0):
            far_copy(front_ref, base + 2 + i, level).start()

    @pl.when(rear)
    def _():
        spread(rear_ref, REAR_PLAN)

    pa_ref[...] = dot(gated_ref[...], out_a[...]).astype(BF16)
    queries_ref[...] = base_ref[:, :width] + scale_b * dot(gated_ref[...], through_ref[:, :width])
    length = float(n * rows)
    weights = resid_ref[...] * jnp.sqrt(
        one_minus_exp(2.0 * rates) / one_minus_exp(2.0 * rates * length)
    )
    modes_over_rows(weights[:, None, :] * jnp.exp(-rates3 * within), step, filt_ref)
    high, low = split(filt_ref[...])
    long_spec = dot(own_f[...], high) + dot(own_f[...], low)
    read = jnp.exp(-rates3 * (within + 1.0))
    two_blocks = jnp.exp(-rates * float(2 * rows))
    four_blocks = jnp.exp(-rates * float(4 * rows))
    seated = jnp.exp(-rates * (place * rows).astype(F32))
    local_ref[...] = dot(back_f[...], spectral_product(dot(own_f[...], signal_ref[...]), long_spec))

    always = size(rim_ref) + size(own_ref)
    letter = size(pair_ref)

    @pl.when(jnp.logical_and(jnp.logical_not(speaks), me < n - 1))
    def _():
        settle(span_ref, send_sem, always)

    @pl.when(me == n - 1)
    def _():
        settle(span_ref, send_sem, size(own_ref))

    for there in range(levels):
        rest = (levels - 1 - there) * QUAD

        @pl.when(jnp.logical_and(front, level == there))
        def _():
            settle(span_ref, send_sem, always + (rest + 2) * letter)

        @pl.when(jnp.logical_and(rear, level == there))
        def _():
            settle(span_ref, send_sem, always + rest * letter)

    def gather(source, total):
        pairs = front_ref[source].astype(F32) * two_blocks
        return total * four_blocks + (pairs + rear_ref[source].astype(F32))

    older = jnp.maximum(level - 1, 0)
    for there in range(2, levels):

        @pl.when(level == there)
        def _():
            settle(span_ref, far_recv.at[0], 2 * (there - 1) * letter)

    total = lax.fori_loop(0, older, gather, jnp.zeros((modes, width), F32))
    back = place >= 2

    @pl.when(jnp.logical_and(level > 0, jnp.logical_not(back)))
    def _():
        settle(span_ref, far_recv.at[1], 2 * letter)

    @pl.when(jnp.logical_and(level > 0, back))
    def _():
        settle(span_ref, far_recv.at[1], 3 * letter)

    @pl.when(jnp.logical_and(level == 0, back))
    def _():
        settle(span_ref, far_recv.at[1], letter)

    total = jnp.where(level > 0, gather(older, total), 0.0) * seated
    pairs = front_ref[level].astype(F32)
    extra = jnp.where(place == 0, 0.0, mate_ref[...])
    extra = jnp.where(place < 2, extra, jnp.where(place == 2, pairs, pairs * block + extra))
    total = total + extra
    modes_over_rows((total * weights)[:, None, :] * read, step, filt_ref)
    long_out = (local_ref[...] + filt_ref[...]).astype(BF16)
    gated_b = (queries_ref[...] * long_out.astype(F32)).astype(BF16)
    pb_ref[...] = dot(gated_b, out_b[...]).astype(BF16)


def solution(mesh):
    n = mesh.shape["seq"]
    assert n % QUAD == 0

    def on_device(*args):
        rows, width = args[0].shape
        modes = args[9].shape[0]
        args = [a[None] if a.ndim == 1 else a for a in args] + dft_tables(rows)
        block = jax.ShapeDtypeStruct((rows, width), BF16)
        span = sum(size(a) for a in args) + (n + 8) * modes * width * 2
        fast = pltpu.VMEM((rows, width), BF16)
        inside = pl.BlockSpec(memory_space=pltpu.VMEM)
        anywhere = pl.BlockSpec(memory_space=pl.ANY)
        results = pl.pallas_call(
            functools.partial(kernel, n),
            out_shape=(fast, fast),
            in_specs=[anywhere] * len(args),
            out_specs=(inside, inside),
            scratch_shapes=[pltpu.VMEM(a.shape, a.dtype) for a in args]
            + [
                pltpu.VMEM((rows, width), BF16),
                pltpu.VMEM((rows, width), BF16),
                pltpu.VMEM((rows, width), F32),
                pltpu.VMEM((rows, width), BF16),
                pltpu.VMEM((rows, width), BF16),
                pltpu.VMEM((modes, width), F32),
                pltpu.VMEM((modes, width), F32),
                pltpu.VMEM((modes, width), BF16),
                pltpu.VMEM((n // QUAD, modes, width), BF16),
                pltpu.VMEM((n // QUAD, modes, width), BF16),
                pltpu.VMEM((span // (4 * LANES), 1, LANES), F32),
                pltpu.VMEM((rows, width), F32),
                pltpu.VMEM((rows, width), F32),
                pltpu.VMEM((rows, 3 * width), F32),
                pltpu.VMEM((width, 3 * width), BF16),
                pltpu.VMEM((rows, width), F32),
                pltpu.SemaphoreType.DMA((4,)),
                pltpu.SemaphoreType.DMA((PIECES,)),
                pltpu.SemaphoreType.DMA,
                pltpu.SemaphoreType.DMA((2,)),
                pltpu.SemaphoreType.REGULAR((2,)),
            ],
            compiler_params=pltpu.CompilerParams(collective_id=0, has_side_effects=True),
        )(*args)
        return pl.pallas_call(
            hand_out,
            out_shape=(block, block),
            in_specs=[inside] * 2,
            out_specs=(anywhere, anywhere),
            scratch_shapes=[
                pltpu.VMEM((2 * rows * width * 2 // (4 * LANES), 1, LANES), F32),
                pltpu.SemaphoreType.DMA,
            ],
        )(*[pltpu.with_memory_space_constraint(r, pltpu.VMEM) for r in results])

    shard = P(("groups", "seq"))
    wide = P(("groups", "seq"), None)
    placed = (wide, shard, P(), P(), P(), P(), shard, P(), P(), P(), P(), P())
    return jax.shard_map(
        on_device, mesh=mesh, in_specs=placed, out_specs=(wide, wide), check_vma=False
    )
```

```python
import functools

import jax
import jax.numpy as jnp
import numpy as np
from jax import lax
from jax.experimental import pallas as pl
from jax.experimental.pallas import tpu as pltpu
from jax.sharding import PartitionSpec as P

MESH = pl.DeviceIdType.MESH
F32 = jnp.float32
BF16 = jnp.bfloat16
SUB = 8
LANES = 128
QUAD = 4
PIECES = 2
FRONT_PLAN = [(None, 0), (3, 0), (1, 0), (2, 0), (0, 0), (None, 1), (3, 1), (1, 1), (2, 1), (0, 1)]
REAR_PLAN = [(None, 0), (None, 1), (1, 1), (1, 0), (0, 0), (0, 1), (3, 1), (3, 0), (2, 1), (2, 0)]


def dft_tables(rows):
    freq = (np.arange(rows) + 0.5)[:, None]
    angle = freq * np.arange(rows)[None, :] * (np.pi / rows)
    cos, sin = np.cos(angle), np.sin(angle)
    sign = np.where(np.arange(rows) % 2 == 0, 1.0, -1.0)[:, None]
    own = np.concatenate([cos, sin], 0)
    behind = np.concatenate([sign * sin, -sign * cos], 0)
    back = own.T / rows
    return [jnp.asarray(t, F32).astype(BF16) for t in (own, behind, back)]


def dot(left, right):
    return jnp.dot(left, right, preferred_element_type=F32)


def split(value):
    high = value.astype(BF16)
    return high, (value - high.astype(F32)).astype(BF16)


def one_minus_exp(a):
    series = 1.0 - a / 9.0
    for k in (8.0, 7.0, 6.0, 5.0, 4.0, 3.0, 2.0):
        series = 1.0 - series * a / k
    return jnp.where(a < 0.5, a * series, 1.0 - jnp.exp(-a))


def column(row):
    rows = row.shape[1]
    eye = lax.broadcasted_iota(jnp.int32, (rows, rows), 0) == lax.broadcasted_iota(
        jnp.int32, (rows, rows), 1
    )
    return jnp.sum(jnp.where(eye, row, 0.0), axis=1, keepdims=True)


def scaled(tokens, scale, gain):
    return (tokens.astype(F32) * scale * gain).astype(BF16)


def spectral_product(data, filt):
    half = data.shape[0] // 2
    dc, ds, fc, fs = data[:half], data[half:], filt[:half], filt[half:]
    return jnp.concatenate([dc * fc - ds * fs, dc * fs + ds * fc], 0).astype(BF16)


def modes_over_rows(first, step, out_ref):
    rows, width = out_ref.shape
    for lane in range(0, width, LANES):
        cols = slice(lane, lane + LANES)
        term, ratio = first[:, :, cols], step[:, :, cols]
        for a in range(rows // SUB):
            out_ref[a * SUB : (a + 1) * SUB, cols] = jnp.sum(term, axis=0)
            if a + 1 < rows // SUB:
                term = term * ratio


def sublane_sums(parts):
    row = lax.broadcasted_iota(jnp.int32, parts[0].shape, 0)
    high = row >= 4
    parts = [
        jnp.where(high, b, a) + pltpu.roll(jnp.where(high, a, b), 4, 0)
        for a, b in zip(parts[:4], parts[4:])
    ]
    for shift in (2, 1):
        odd = lax.rem(row // shift, 2) == 1
        count = len(parts) // 2
        parts = [
            jnp.where(odd, b + pltpu.roll(b, shift, 0), a + pltpu.roll(a, SUB - shift, 0))
            for a, b in zip(parts[:count], parts[count:])
        ]
    return parts[0]


def end_totals(totals, signal, step):
    rows, width = signal.shape
    modes = step.shape[0]
    sums = {}
    for lane in range(0, width, LANES):
        cols = slice(lane, lane + LANES)
        tiles = [signal[r : r + SUB, cols] for r in range(0, rows, SUB)]
        for m in range(modes):
            total, rest = (tiles[0], tiles[1:]) if totals is None else (totals[lane, m], tiles)
            for tile in rest:
                total = total * step[m, :, cols] + tile
            sums[lane, m] = total
    return sums


def end_state(totals, last):
    modes, _, width = last.shape
    columns = []
    for lane in range(0, width, LANES):
        parts = [totals[lane, m] * last[m, :, lane : lane + LANES] for m in range(modes)]
        columns.append(
            jnp.concatenate([sublane_sums(parts[m : m + SUB]) for m in range(0, modes, SUB)], 0)
        )
    return jnp.concatenate(columns, 1)


def size(ref):
    return int(np.prod(ref.shape)) * ref.dtype.itemsize


def settle(span_ref, sem, total):
    part = span_ref.at[pl.ds(0, total // (LANES * 4))]
    pltpu.make_async_copy(part, part, sem).wait()


def hand_out(a_ref, b_ref, pa_ref, pb_ref, span_ref, sem):
    copies = [
        pltpu.make_async_copy(a_ref, pa_ref, sem),
        pltpu.make_async_copy(b_ref, pb_ref, sem),
    ]
    for copy in copies:
        copy.start()
    settle(span_ref, sem, size(a_ref) + size(b_ref))


def kernel(n, *refs):
    hbm = refs[:15]
    pa_ref, pb_ref = refs[15:17]
    vm = refs[17:32]
    (tail_ref, rim_ref, filt_ref, signal_ref, gated_ref) = refs[32:37]
    (own_ref, mate_ref, pair_ref, front_ref, rear_ref, span_ref) = refs[37:43]
    (queries_ref, short_ref, base_ref, through_ref, local_ref) = refs[43:48]
    (load_sem, rim_recv, mate_recv, far_recv, far_sem) = refs[48:]
    send_sem = load_sem.at[2]
    rows, width = vm[0].shape
    modes = vm[9].shape[0]

    groups = ((1, 2, 0), (3,), (12, 4, 13, 14), (15, 9, 10, 5, 6, 7, 8, 11))
    pairs_of = dict(enumerate(zip(hbm, vm)))
    keys = (slice(None), pl.ds(width, 2 * width))
    queries_only = (slice(None), pl.ds(0, width))
    pairs_of[3] = (hbm[3].at[keys], vm[3].at[keys])
    pairs_of[15] = (hbm[3].at[queries_only], vm[3].at[queries_only])
    loads = [
        [pltpu.make_async_copy(*pairs_of[i], load_sem.at[g]) for i in group]
        for g, group in enumerate(groups)
    ]

    def start(*which):
        for g in which:
            for load in loads[g]:
                load.start()

    def arrive(g):
        settle(span_ref, load_sem.at[g], sum(size(pairs_of[i][1]) for i in groups[g]))

    start(0, 1)
    me = lax.axis_index("seq")

    levels = n // QUAD
    level, place = me // QUAD, lax.rem(me, QUAD)
    base = level * QUAD
    mate = me + 1 - 2 * lax.rem(me, 2)
    speaker = (level == 0).astype(jnp.int32)
    front = place == speaker
    rear = place == 2
    speaks = jnp.logical_or(front, rear)
    barrier = pltpu.get_barrier_semaphore()

    def signal(sem, target):
        pl.semaphore_signal(sem, inc=1, device_id={"seq": target}, device_id_type=MESH)

    @pl.when(jnp.logical_and(place == 0, level > 0))
    def _():
        signal(barrier, me - 1)

    for i in range(1, QUAD):
        signal(barrier, base + lax.rem(place + QUAD - i, QUAD))

    @pl.when(speaks)
    def _():
        @pl.loop(level + 1, levels)
        def _(i):
            signal(barrier, i * QUAD + 2)

    start(2)
    (tok, rms_a, gain_a, proj_a, taps, out_a) = vm[:6]
    (rms_b, gain_b, proj_b, rates_ref, resid_ref, out_b, own_f, rim_f, back_f) = vm[6:]

    cut = rows * 5 // 8
    spans = ((0, cut), (cut, rows))
    pieces = [pl.ds(a, b - a) for a, b in spans]

    @pl.when(me == 0)
    def _():
        gated_ref[...] = jnp.zeros_like(gated_ref)
        for i, p in enumerate(pieces):
            pltpu.make_async_copy(gated_ref.at[p], rim_ref.at[p], rim_recv.at[i]).start()

    crossing = jnp.logical_and(place == QUAD - 1, level < levels - 1)

    @pl.when(rear)
    def _():
        pl.semaphore_wait(barrier, QUAD - 1 + 2 * level)

        @pl.loop(0, level)
        def _(i):
            credit = far_sem.at[(level == levels - 1).astype(jnp.int32)]
            signal(credit, i * QUAD + 2)
            signal(credit, i * QUAD + (i == 0).astype(jnp.int32))

    arrive(0)
    normed = scaled(tok[...], column(rms_a[...]), gain_a[...])
    arrive(1)
    start(3)
    pair_a = dot(normed, proj_a[:, width:])
    product = (pair_a[:, :width] * pair_a[:, width:]).astype(BF16)
    arrive(2)
    taps_spec = dot(own_f[...], taps[...])
    tail_ref[...] = dot(
        back_f[...], spectral_product(dot(rim_f[...], product), taps_spec)
    ).astype(BF16)

    @pl.when(jnp.logical_not(rear))
    def _():
        pl.semaphore_wait(barrier, QUAD - 1 + crossing.astype(jnp.int32))

    rim_copies = [
        pltpu.make_async_remote_copy(
            src_ref=tail_ref.at[p],
            dst_ref=rim_ref.at[p],
            send_sem=send_sem,
            recv_sem=rim_recv.at[i],
            device_id={"seq": lax.rem(me + 1, n)},
            device_id_type=MESH,
        )
        for i, p in enumerate(pieces)
    ]

    @pl.when(me < n - 1)
    def _():
        for copy in rim_copies:
            copy.start()

    arrive(3)
    queries_ref[...] = dot(normed, proj_a[:, :width])
    short_ref[...] = dot(back_f[...], spectral_product(dot(own_f[...], product), taps_spec))

    rates = rates_ref[...]
    length = float(n * rows)
    rates3 = jnp.broadcast_to(rates[:, None, :], (modes, SUB, width))
    within = lax.broadcasted_iota(jnp.int32, (modes, SUB, width), 1).astype(F32)
    step = jnp.exp(-rates3 * float(SUB))
    last = jnp.exp(-rates3 * (SUB - 1.0 - within))
    block = jnp.exp(-rates * float(rows))
    scale_b = column(rms_b[...])
    base_ref[...] = dot(scaled(tok[...], scale_b, gain_b[...]), proj_b[...])
    high, low = split(out_a[...].astype(F32) * gain_b[...])
    through_ref[...] = (dot(high, proj_b[...]) + dot(low, proj_b[...])).astype(BF16)

    totals = None
    for i, p in enumerate(pieces):
        rim_copies[i].wait_recv()
        span = slice(*spans[i])
        gated = (queries_ref[p] * (short_ref[p] + rim_ref[p].astype(F32))).astype(BF16)
        gated_ref[p] = gated
        pair_b = base_ref[p, width:] + scale_b[span] * dot(gated, through_ref[:, width:])
        signal = (pair_b[:, :width] * pair_b[:, width:]).astype(BF16)
        signal_ref[p] = signal
        totals = end_totals(totals, signal.astype(F32), step)
    state = end_state(totals, last)
    own_ref[...] = state

    mate_copy = pltpu.make_async_remote_copy(
        src_ref=own_ref,
        dst_ref=mate_ref,
        send_sem=send_sem,
        recv_sem=mate_recv,
        device_id={"seq": mate},
        device_id_type=MESH,
    )
    mate_copy.start()

    def far_copy(slots, target, there):
        return pltpu.make_async_remote_copy(
            src_ref=pair_ref,
            dst_ref=slots.at[level],
            send_sem=send_sem,
            recv_sem=far_recv.at[(there - level <= 1).astype(jnp.int32)],
            device_id={"seq": target},
            device_id_type=MESH,
        )

    mate_copy.wait_recv()
    early = lax.rem(place, 2) == 0
    pair_ref[...] = (
        jnp.where(early, state, mate_ref[...]) * block + jnp.where(early, mate_ref[...], state)
    ).astype(BF16)

    def spread(slots, plan):
        for seat_there, last_level in plan:
            if seat_there is None:

                @pl.when(level < levels - (1 if last_level else 2))
                def _():
                    if last_level:
                        pl.semaphore_wait(far_sem.at[1], 1)
                    else:
                        pl.semaphore_wait(far_sem.at[0], levels - 2 - level)

            elif last_level:

                @pl.when(level < levels - 1)
                def _():
                    far_copy(slots, (levels - 1) * QUAD + seat_there, levels - 1).start()

            else:

                @pl.loop(level + 1, levels - 1)
                def _(there):
                    far_copy(slots, there * QUAD + seat_there, there).start()

    @pl.when(front)
    def _():
        spread(front_ref, FRONT_PLAN)
        for i in (1, 0):
            far_copy(front_ref, base + 2 + i, level).start()

    @pl.when(rear)
    def _():
        spread(rear_ref, REAR_PLAN)

    pa_ref[...] = dot(gated_ref[...], out_a[...]).astype(BF16)
    queries_ref[...] = base_ref[:, :width] + scale_b * dot(gated_ref[...], through_ref[:, :width])
    length = float(n * rows)
    weights = resid_ref[...] * jnp.sqrt(
        one_minus_exp(2.0 * rates) / one_minus_exp(2.0 * rates * length)
    )
    modes_over_rows(weights[:, None, :] * jnp.exp(-rates3 * within), step, filt_ref)
    high, low = split(filt_ref[...])
    long_spec = dot(own_f[...], high) + dot(own_f[...], low)
    read = jnp.exp(-rates3 * (within + 1.0))
    two_blocks = jnp.exp(-rates * float(2 * rows))
    four_blocks = jnp.exp(-rates * float(4 * rows))
    seated = jnp.exp(-rates * (place * rows).astype(F32))
    local_ref[...] = dot(back_f[...], spectral_product(dot(own_f[...], signal_ref[...]), long_spec))

    always = size(rim_ref) + size(own_ref)
    letter = size(pair_ref)

    @pl.when(jnp.logical_and(jnp.logical_not(speaks), me < n - 1))
    def _():
        settle(span_ref, send_sem, always)

    @pl.when(me == n - 1)
    def _():
        settle(span_ref, send_sem, size(own_ref))

    for there in range(levels):
        rest = (levels - 1 - there) * QUAD

        @pl.when(jnp.logical_and(front, level == there))
        def _():
            settle(span_ref, send_sem, always + (rest + 2) * letter)

        @pl.when(jnp.logical_and(rear, level == there))
        def _():
            settle(span_ref, send_sem, always + rest * letter)

    def gather(source, total):
        pairs = front_ref[source].astype(F32) * two_blocks
        return total * four_blocks + (pairs + rear_ref[source].astype(F32))

    older = jnp.maximum(level - 1, 0)
    for there in range(2, levels):

        @pl.when(level == there)
        def _():
            settle(span_ref, far_recv.at[0], 2 * (there - 1) * letter)

    total = lax.fori_loop(0, older, gather, jnp.zeros((modes, width), F32))
    back = place >= 2

    @pl.when(jnp.logical_and(level > 0, jnp.logical_not(back)))
    def _():
        settle(span_ref, far_recv.at[1], 2 * letter)

    @pl.when(jnp.logical_and(level > 0, back))
    def _():
        settle(span_ref, far_recv.at[1], 3 * letter)

    @pl.when(jnp.logical_and(level == 0, back))
    def _():
        settle(span_ref, far_recv.at[1], letter)

    total = jnp.where(level > 0, gather(older, total), 0.0) * seated
    pairs = front_ref[level].astype(F32)
    extra = jnp.where(place == 0, 0.0, mate_ref[...])
    extra = jnp.where(place < 2, extra, jnp.where(place == 2, pairs, pairs * block + extra))
    total = total + extra
    modes_over_rows((total * weights)[:, None, :] * read, step, filt_ref)
    long_out = (local_ref[...] + filt_ref[...]).astype(BF16)
    gated_b = (queries_ref[...] * long_out.astype(F32)).astype(BF16)
    pb_ref[...] = dot(gated_b, out_b[...]).astype(BF16)


def solution(mesh):
    n = mesh.shape["seq"]
    assert n % QUAD == 0

    def on_device(*args):
        rows, width = args[0].shape
        modes = args[9].shape[0]
        args = [a[None] if a.ndim == 1 else a for a in args] + dft_tables(rows)
        block = jax.ShapeDtypeStruct((rows, width), BF16)
        span = sum(size(a) for a in args) + (n + 8) * modes * width * 2
        fast = pltpu.VMEM((rows, width), BF16)
        inside = pl.BlockSpec(memory_space=pltpu.VMEM)
        anywhere = pl.BlockSpec(memory_space=pl.ANY)
        results = pl.pallas_call(
            functools.partial(kernel, n),
            out_shape=(fast, fast),
            in_specs=[anywhere] * len(args),
            out_specs=(inside, inside),
            scratch_shapes=[pltpu.VMEM(a.shape, a.dtype) for a in args]
            + [
                pltpu.VMEM((rows, width), BF16),
                pltpu.VMEM((rows, width), BF16),
                pltpu.VMEM((rows, width), F32),
                pltpu.VMEM((rows, width), BF16),
                pltpu.VMEM((rows, width), BF16),
                pltpu.VMEM((modes, width), F32),
                pltpu.VMEM((modes, width), F32),
                pltpu.VMEM((modes, width), BF16),
                pltpu.VMEM((n // QUAD, modes, width), BF16),
                pltpu.VMEM((n // QUAD, modes, width), BF16),
                pltpu.VMEM((span // (4 * LANES), 1, LANES), F32),
                pltpu.VMEM((rows, width), F32),
                pltpu.VMEM((rows, width), F32),
                pltpu.VMEM((rows, 3 * width), F32),
                pltpu.VMEM((width, 3 * width), BF16),
                pltpu.VMEM((rows, width), F32),
                pltpu.SemaphoreType.DMA((4,)),
                pltpu.SemaphoreType.DMA((PIECES,)),
                pltpu.SemaphoreType.DMA,
                pltpu.SemaphoreType.DMA((2,)),
                pltpu.SemaphoreType.REGULAR((2,)),
            ],
            compiler_params=pltpu.CompilerParams(collective_id=0, has_side_effects=True),
        )(*args)
        return pl.pallas_call(
            hand_out,
            out_shape=(block, block),
            in_specs=[inside] * 2,
            out_specs=(anywhere, anywhere),
            scratch_shapes=[
                pltpu.VMEM((2 * rows * width * 2 // (4 * LANES), 1, LANES), F32),
                pltpu.SemaphoreType.DMA,
            ],
        )(*[pltpu.with_memory_space_constraint(r, pltpu.VMEM) for r in results])

    shard = P(("groups", "seq"))
    wide = P(("groups", "seq"), None)
    placed = (wide, shard, P(), P(), P(), P(), shard, P(), P(), P(), P(), P())
    return jax.shard_map(
        on_device, mesh=mesh, in_specs=placed, out_specs=(wide, wide), check_vma=False
    )
```
